128 devices in a mesh: ctx: 32 (over x, z, core), tp: 4 (over y).
Axes of the slice: x: 4, y: 4, z: 4, core: 2. Of those that a mesh axis runs over, the one named last changes fastest.
Arguments:
- queries: bfloat16 [16384, 5120], P(('ctx', 'tp')), may hold values from -400 to 400
- keys: bfloat16 [16384, 5120], P(('ctx', 'tp')), may hold values from -6 to 6
- values: bfloat16 [16384, 5120], P(('ctx', 'tp')), may hold values from -6 to 6
- dout: bfloat16 [16384, 5120], P(('ctx', 'tp')), may hold values from -6 to 6
- match: int32 [10, 64], replicated, may hold values from 0 to 63, as said below
Outputs:
- attended: bfloat16 [16384, 5120], P(('ctx', 'tp'))
- grad_queries: bfloat16 [16384, 5120], P(('ctx', 'tp'))
- grad_keys: bfloat16 [16384, 5120], P(('ctx', 'tp'))
- grad_values: bfloat16 [16384, 5120], P(('ctx', 'tp'))
The draws below stay inside these ranges and needn't reach their ends.
Inputs may be any that keep to these rules, and one draw needn't show every extreme that they name: match[g, i] lies in 0 to i; the value i means that query block i has no matched block for group g. Among the 20 pairs of a query block and a group of one ctx index, at most 1 name a block of the tokens of any one other ctx index, and 1 is reached.
All inputs are finite; a program needn't handle non-finite values.
Results may differ from the reference program's by a relative error of at most 0.025.
Values may be sent and summed in bfloat16 or wider, within the bound.
No kernel may reach another device: no remote copies, remote signals or barrier semaphores. Data moves between devices by JAX's collectives and lax.ppermute only.
A program may use at most 128 MiB of HBM per device.

```python
import jax
import jax.numpy as jnp
from jax import lax

HEADS = 40
HEAD_DIM = 128
BLOCK = 256
GROUPS = 10
CAP = 1
SEQ = 16384
NB = 64
NB_DEV = 2
WIDTH = 5120


def draw_match(key, part):
    total_blocks = NB
    per_device = NB_DEV
    ctx_count = NB // NB_DEV
    block_ids = jnp.arange(total_blocks, dtype=jnp.int32)
    target = block_ids // per_device
    position = block_ids % per_device
    first_draw = jax.random.randint(jax.random.fold_in(key, 1), (GROUPS, total_blocks), 0, 1 << 20, dtype=jnp.int32)
    second_draw = jax.random.randint(jax.random.fold_in(key, 2), (GROUPS, total_blocks), 0, 1 << 20, dtype=jnp.int32)
    third_draw = jax.random.randint(jax.random.fold_in(key, 3), (GROUPS, total_blocks), 0, 1 << 20, dtype=jnp.int32)
    span_size = target + 1
    source = first_draw % span_size * (second_draw % span_size) // jnp.maximum(target, 1)
    local_pick = target * per_device + third_draw % jnp.maximum(position, 1)
    local_pick = jnp.where(position > 0, local_pick, block_ids)
    far_pick = source * per_device + third_draw % per_device
    remote = source < target
    source_t = source.T.reshape(ctx_count, per_device * GROUPS)
    remote_t = remote.T.reshape(ctx_count, per_device * GROUPS)
    onehot = ((source_t[:, :, None] == jnp.arange(ctx_count, dtype=jnp.int32)) & remote_t[:, :, None]).astype(jnp.int32)
    before = jnp.cumsum(onehot, axis=1) - onehot
    slot_rank = jnp.sum(before * onehot, axis=2)
    kept_t = remote_t & (slot_rank < CAP)
    kept = kept_t.reshape(total_blocks, GROUPS).T
    chosen = jnp.where(remote, jnp.where(kept, far_pick, block_ids), local_pick)
    group_ids = jnp.arange(GROUPS, dtype=jnp.int32)
    last_mark = (group_ids[:, None] == 0) & (block_ids[None, :] == total_blocks - 1)
    chosen = jnp.where(last_mark, block_ids[None, :], chosen)
    return chosen.astype(jnp.int32)


def base_keys(key):
    noise = jax.random.normal(jax.random.fold_in(key, 7), (SEQ, HEADS * HEAD_DIM), jnp.float32)
    return jnp.clip(noise, -6.0, 6.0)


def draw_keys(key, part):
    basis = base_keys(key)
    return basis.astype(jnp.bfloat16)


def draw_queries(key, part):
    fresh = jnp.clip(jax.random.normal(jax.random.fold_in(key, 8), (SEQ, HEADS * HEAD_DIM), jnp.float32), -6.0, 6.0)
    return fresh.astype(jnp.bfloat16)


def shard_levels(own_key, shape, split, least, largest):
    factor_of = 1.0
    for axis_at, blocks in split:
        steps = jax.random.uniform(jax.random.fold_in(jax.random.fold_in(own_key, 6), axis_at), (blocks,), jnp.float32, least / len(split), largest / len(split))
        factor_of = factor_of * jnp.repeat(jnp.exp(steps), shape[axis_at] // blocks).reshape((-1,) + (1,) * (len(shape) - 1 - axis_at))
    return factor_of


def normal_values(rng, shape, deviation, bound, split=(), held_as=jnp.bfloat16):
    entries = deviation * jax.random.normal(rng, shape, jnp.float32)
    if split:
        entries = entries * shard_levels(rng, shape, split, -0.22, 0.18)
    return jnp.clip(entries, -bound, bound).astype(held_as)


def setup_inputs(seed: int = 0) -> dict:
    seeds = jax.random.split(jax.random.key(seed), 6)
    queries = draw_queries(jax.random.fold_in(seeds[5], 71), 0)
    keys = draw_keys(jax.random.fold_in(seeds[5], 71), 0)
    values = normal_values(seeds[2], (SEQ, WIDTH), 1.0, 6.0, ((0, 128),))
    dout = normal_values(seeds[3], (SEQ, WIDTH), 1.0, 6.0, ((0, 128),))
    match = draw_match(jax.random.fold_in(seeds[5], 71), 0)
    return {"queries": queries, "keys": keys, "values": values, "dout": dout, "match": match}


def reference(queries, keys, values, dout, match):
    score_scale = HEAD_DIM ** -0.5
    total_blocks = queries.shape[0] // BLOCK

    def split_blocks(array):
        return array.reshape(total_blocks, BLOCK, HEADS, HEAD_DIM)

    q_all = split_blocks(queries)
    k_all = split_blocks(keys)
    v_all = split_blocks(values)
    d_all = split_blocks(dout)
    head_ids = jnp.arange(HEADS, dtype=jnp.int32)
    head_match = match[head_ids % GROUPS, :]
    causal = jnp.arange(BLOCK)[:, None] >= jnp.arange(BLOCK)[None, :]

    def to_bf16_f32(array):
        rounded = lax.optimization_barrier(array.astype(jnp.bfloat16))
        return rounded.astype(jnp.float32)

    def step(carry, index):
        acc_k, acc_v = carry
        q_blk = lax.dynamic_index_in_dim(q_all, index, 0, keepdims=False).astype(jnp.float32)
        k_own = lax.dynamic_index_in_dim(k_all, index, 0, keepdims=False).astype(jnp.float32)
        v_own = lax.dynamic_index_in_dim(v_all, index, 0, keepdims=False).astype(jnp.float32)
        d_blk = lax.dynamic_index_in_dim(d_all, index, 0, keepdims=False).astype(jnp.float32)
        partner = lax.dynamic_index_in_dim(head_match, index, 1, keepdims=False)
        is_valid = partner < index
        far_k = k_all[partner, :, head_ids, :].astype(jnp.float32)
        far_v = v_all[partner, :, head_ids, :].astype(jnp.float32)
        s_own = jnp.einsum('qhd,khd->hqk', q_blk, k_own) * score_scale
        s_own = jnp.where(causal[None], s_own, -jnp.inf)
        s_far = jnp.einsum('qhd,hkd->hqk', q_blk, far_k) * score_scale
        s_far = jnp.where(is_valid[:, None, None], s_far, -jnp.inf)
        row_top = jnp.maximum(jnp.max(s_own, axis=-1), jnp.max(s_far, axis=-1))
        row_total = jnp.sum(jnp.exp(s_own - row_top[..., None]), axis=-1) + jnp.sum(jnp.exp(s_far - row_top[..., None]), axis=-1)
        log_total = row_top + jnp.log(row_total)
        p_own = jnp.exp(s_own - log_total[..., None])
        p_far = jnp.exp(s_far - log_total[..., None])
        pb_own = to_bf16_f32(p_own)
        pb_far = to_bf16_f32(p_far)
        attended = jnp.einsum('hqk,khd->qhd', pb_own, v_own) + jnp.einsum('hqk,hkd->qhd', pb_far, far_v)
        out_blk = attended.astype(jnp.bfloat16)
        delta = jnp.sum(d_blk * out_blk.astype(jnp.float32), axis=-1).T
        dp_own = jnp.einsum('qhd,khd->hqk', d_blk, v_own)
        dp_far = jnp.einsum('qhd,hkd->hqk', d_blk, far_v)
        ds_own = to_bf16_f32(p_own * (dp_own - delta[..., None]) * score_scale)
        ds_far = to_bf16_f32(p_far * (dp_far - delta[..., None]) * score_scale)
        grad_q = jnp.einsum('hqk,khd->qhd', ds_own, k_own) + jnp.einsum('hqk,hkd->qhd', ds_far, far_k)
        gk_own = jnp.einsum('hqk,qhd->khd', ds_own, q_blk)
        gv_own = jnp.einsum('hqk,qhd->khd', pb_own, d_blk)
        gk_far = jnp.einsum('hqk,qhd->hkd', ds_far, q_blk)
        gv_far = jnp.einsum('hqk,qhd->hkd', pb_far, d_blk)
        acc_k = acc_k.at[index].add(gk_own)
        acc_v = acc_v.at[index].add(gv_own)
        acc_k = acc_k.at[partner, :, head_ids, :].add(gk_far)
        acc_v = acc_v.at[partner, :, head_ids, :].add(gv_far)
        return (acc_k, acc_v), (out_blk, grad_q.astype(jnp.bfloat16))

    zeros_acc = jnp.zeros((total_blocks, BLOCK, HEADS, HEAD_DIM), jnp.float32)
    (acc_k, acc_v), (outs, grads_q) = lax.scan(step, (zeros_acc, zeros_acc), jnp.arange(total_blocks, dtype=jnp.int32))
    full_shape = (total_blocks * BLOCK, HEADS * HEAD_DIM)
    return (outs.reshape(full_shape), grads_q.reshape(full_shape), acc_k.astype(jnp.bfloat16).reshape(full_shape), acc_v.astype(jnp.bfloat16).reshape(full_shape))
```

```python
import jax
import jax.numpy as jnp
from jax import lax
from jax.experimental import pallas as pl
from jax.experimental.pallas import tpu as pltpu
from jax.sharding import PartitionSpec as P


HEAD_DIM = 128
BLOCK = 256
GROUPS = 10
CTX = 32
TP = 4
TOK = 128
ROWS = TP * TOK
COLS = GROUPS * HEAD_DIM
SCALE = HEAD_DIM ** (-0.5)
F32 = jnp.float32
BF16 = jnp.bfloat16


ANY = pl.BlockSpec(memory_space=pl.ANY)
SMEM = pl.BlockSpec(memory_space=pltpu.SMEM)
VMEM = pl.BlockSpec(memory_space=pltpu.VMEM)
HBM = pl.BlockSpec(memory_space=pltpu.HBM)


ITEMS = 2 * GROUPS
PARAMS = pltpu.CompilerParams(vmem_limit_bytes=40 * 1024 * 1024)


def shape(dims, dtype=BF16):
    return jax.ShapeDtypeStruct(dims, dtype)


def peer(step):
    return lax.rem(lax.axis_index("tp") + step, TP)


def col_slice(index):
    return pl.ds(pl.multiple_of(index * COLS, COLS), COLS)


def row_slice(index):
    return pl.ds(pl.multiple_of(index * TOK, TOK), TOK)


def block_slice(index):
    return pl.ds(pl.multiple_of(index * BLOCK, BLOCK), BLOCK)


def head_slice(index):
    return pl.ds(pl.multiple_of(index * HEAD_DIM, HEAD_DIM), HEAD_DIM)


def call(kernel, out_shape, in_specs, out_specs, scratch):
    def run(*operands):
        return pl.pallas_call(
            kernel,
            out_shape=out_shape,
            in_specs=in_specs,
            out_specs=out_specs,
            scratch_shapes=scratch,
            compiler_params=PARAMS,
        )(*operands)

    return run


def run_copies(copies):
    for copy in copies:
        copy.start()
    for copy in copies:
        copy.wait()


def cut_kernel(a_ref, b_ref, p1, p2, p3, sems):
    copies = []
    for step, out in ((1, p1), (2, p2), (3, p3)):
        for which, ref in enumerate((a_ref, b_ref)):
            copies.append(
                pltpu.make_async_copy(
                    ref.at[:, col_slice(peer(step))], out.at[which], sems.at[len(copies)]
                )
            )
    run_copies(copies)


def cut(a, b):
    return call(
        cut_kernel,
        [shape((2, TOK, COLS))] * 3,
        [HBM] * 2,
        [VMEM] * 3,
        [pltpu.SemaphoreType.DMA((6,))],
    )(a, b)


def join_kernel(own, r1, r2, r3, out, sems):
    copies = []
    for step, ref in ((0, own), (1, r1), (2, r2), (3, r3)):
        copies.append(
            pltpu.make_async_copy(ref, out.at[:, col_slice(peer(TP - step))], sems.at[step])
        )
    run_copies(copies)


def join(own, received):
    return call(
        join_kernel, shape((TOK, TP * COLS)), [VMEM] * 4, HBM, [pltpu.SemaphoreType.DMA((4,))]
    )(own, *received)


def exchange(pieces):
    received = []
    for step, piece in zip((1, 2, 3), pieces):
        received.append(
            lax.ppermute(piece, "tp", [(i, (i + step) % TP) for i in range(TP)])
        )
    return tuple(received)


def gather_copies(a_ref, b_ref, received, held, sems, base):
    copies = []
    for which, ref in enumerate((a_ref, b_ref)):
        copies.append(
            pltpu.make_async_copy(
                ref.at[:, col_slice(peer(0))],
                held.at[which, row_slice(peer(0))],
                sems.at[base + len(copies)],
            )
        )
    for step, ref in zip((1, 2, 3), received):
        for which in range(2):
            copies.append(
                pltpu.make_async_copy(
                    ref.at[which],
                    held.at[which, row_slice(peer(TP - step))],
                    sems.at[base + len(copies)],
                )
            )
    return copies


def table_kernel(match, tab):
    ctx = lax.axis_index("ctx")

    def clear(d, carry):
        for row in range(5):
            tab[row, d] = 0
        return carry

    lax.fori_loop(0, CTX, clear, 0)

    def owner_side(d, carry):
        for n in range(2):
            for g in range(GROUPS):
                block = 2 * d + n
                m = match[g, block]

                @pl.when((m < block) & ((m >> 1) == ctx))
                def _():
                    tab[0, d] = m & 1
                    tab[1, d] = g
                    tab[2, d] = 1

        return carry

    lax.fori_loop(ctx + 1, CTX, owner_side, 0)
    for n in range(2):
        for g in range(GROUPS):
            block = 2 * ctx + n
            m = match[g, block]
            source = m >> 1
            item = n * GROUPS + g

            @pl.when((m < block) & (source != ctx))
            def _():
                tab[0, source] = n
                tab[1, source] = g
                tab[2, source] = 1
                tab[3, item] = 1
                tab[4, item] = source

            @pl.when((m < block) & (source == ctx))
            def _():
                tab[3, item] = 2


def make_table(match):
    return call(table_kernel, shape((8, CTX), jnp.int32), [SMEM], SMEM, [])(match)


def pack_kernel(tab, a_ref, b_ref, r1, r2, r3, out, held_out, held, sems, slot_sems):
    ctx = lax.axis_index("ctx")
    run_copies(gather_copies(a_ref, b_ref, (r1, r2, r3), held, sems, 0))
    copies = []
    for d in range(CTX):
        which = jnp.where(ctx > d, 1, 0)
        copies.append(
            pltpu.make_async_copy(
                held.at[which, block_slice(tab[0, d]), head_slice(tab[1, d])],
                out.at[d],
                slot_sems.at[d],
            )
        )
    copies.append(pltpu.make_async_copy(held, held_out, slot_sems.at[CTX]))
    run_copies(copies)


def pack(tab, a, b, received):
    return call(
        pack_kernel,
        [shape((CTX, BLOCK, HEAD_DIM)), shape((2, ROWS, COLS))],
        [SMEM] + [HBM] * 2 + [ANY] * 3,
        [HBM] * 2,
        [
            pltpu.VMEM((2, ROWS, COLS), BF16),
            pltpu.SemaphoreType.DMA((8,)),
            pltpu.SemaphoreType.DMA((CTX + 1,)),
        ],
    )(tab, a, b, *received)


def swap(slots):
    return lax.all_to_all(slots, "ctx", split_axis=0, concat_axis=0, tiled=True)


def dot(a, b):
    return lax.dot_general(a, b, (((1,), (0,)), ((), ())), preferred_element_type=F32)


def dot_t(a, b):
    return lax.dot_general(a, b, (((1,), (1,)), ((), ())), preferred_element_type=F32)


def far_copies(tab, slots, far, sems):
    return [
        pltpu.make_async_copy(slots.at[tab[4, item]], far.at[item], sems.at[item])
        for item in range(ITEMS)
    ]


def fill_local(tab, far, held):
    def local(g, carry):
        @pl.when(tab[3, GROUPS + g] == 2)
        def _():
            far[GROUPS + g] = held[pl.ds(0, BLOCK), head_slice(g)]

        return carry

    lax.fori_loop(0, GROUPS, local, 0)


def start_all(copies):
    for copy in copies:
        copy.start()


def wait_all(copies):
    for copy in copies:
        copy.wait()


def prob_kernel(tab, kq_ref, slots, prob_out, lse_out, kq, far, prob, sems, far_sems, out_sems):
    loads = [pltpu.make_async_copy(kq_ref, kq, sems.at[0])]
    loads += far_copies(tab, slots, far, far_sems)
    run_copies(loads)
    fill_local(tab, far, kq.at[0])
    causal = lax.broadcasted_iota(jnp.int32, (BLOCK, BLOCK), 0) >= lax.broadcasted_iota(
        jnp.int32, (BLOCK, BLOCK), 1
    )

    def store(item):
        return pltpu.make_async_copy(prob.at[item], prob_out.at[item], out_sems.at[item])

    def step(g, carry):
        cols = head_slice(g)
        for n in range(2):
            rows = pl.ds(n * BLOCK, BLOCK)
            item = n * GROUPS + g
            q = kq[1, rows, cols]
            s_own = jnp.where(causal, dot_t(q, kq[0, rows, cols]) * SCALE, -jnp.inf)
            s_far = jnp.where(tab[3, item] > 0, dot_t(q, far[item]) * SCALE, -jnp.inf)
            top = jnp.maximum(
                jnp.max(s_own, axis=1, keepdims=True), jnp.max(s_far, axis=1, keepdims=True)
            )
            e_own = jnp.exp(s_own - top)
            e_far = jnp.exp(s_far - top)
            total = jnp.sum(e_own, axis=1, keepdims=True) + jnp.sum(e_far, axis=1, keepdims=True)
            inverse = 1.0 / total
            prob[item, :, pl.ds(0, BLOCK)] = (e_own * inverse).astype(BF16)
            prob[item, :, pl.ds(BLOCK, BLOCK)] = (e_far * inverse).astype(BF16)
            lse = jnp.broadcast_to(top + jnp.log(total), (BLOCK, HEAD_DIM))
            lse_out[item] = jnp.transpose(lse)[0:8]
        for n in range(2):
            store(n * GROUPS + g).start()
        return carry

    lax.fori_loop(0, GROUPS, step, 0)
    wait_all([store(item) for item in range(ITEMS)])


def prob_side(tab, kq, slots):
    return call(
        prob_kernel,
        [shape((ITEMS, BLOCK, 2 * BLOCK)), shape((ITEMS, 8, BLOCK), F32)],
        [SMEM, HBM, HBM],
        [HBM, VMEM],
        [
            pltpu.VMEM((2, ROWS, COLS), BF16),
            pltpu.VMEM((ITEMS, BLOCK, HEAD_DIM), BF16),
            pltpu.VMEM((ITEMS, BLOCK, 2 * BLOCK), BF16),
            pltpu.SemaphoreType.DMA((1,)),
            pltpu.SemaphoreType.DMA((ITEMS,)),
            pltpu.SemaphoreType.DMA((ITEMS,)),
        ],
    )(tab, kq, slots)


def piece_copies(result, outs, sems):
    return [
        pltpu.make_async_copy(result.at[row_slice(peer(move))], out, sems.at[move])
        for move, out in enumerate(outs)
    ]


def prob_copy(prob_ref, prob, item, sems):
    return pltpu.make_async_copy(prob_ref.at[item], prob.at[item], sems.at[item])


def start_probs(prob_ref, prob, sems):
    for g in range(GROUPS):
        for n in range(2):
            prob_copy(prob_ref, prob, n * GROUPS + g, sems).start()


def value_kernel(
    tab, prob_ref, vd_ref, slots, own, p1, p2, p3, full,
    prob, v, far, result, sems, far_sems, prob_sems, out_sems,
):
    loads = [pltpu.make_async_copy(vd_ref.at[0], v, sems.at[0])]
    loads += far_copies(tab, slots, far, far_sems)
    start_all(loads)
    start_probs(prob_ref, prob, prob_sems)
    wait_all(loads)
    fill_local(tab, far, v)

    def step(g, carry):
        cols = head_slice(g)
        for n in range(2):
            prob_copy(prob_ref, prob, n * GROUPS + g, prob_sems).wait()
        for n in range(2):
            rows = pl.ds(n * BLOCK, BLOCK)
            item = n * GROUPS + g
            att = dot(prob[item, :, pl.ds(0, BLOCK)], v[rows, cols])
            att = att + dot(prob[item, :, pl.ds(BLOCK, BLOCK)], far[item])
            result[rows, cols] = att.astype(BF16)
        return carry

    lax.fori_loop(0, GROUPS, step, 0)
    run_copies(
        piece_copies(result, (own, p1, p2, p3), out_sems)
        + [pltpu.make_async_copy(result, full, out_sems.at[TP])]
    )


def value_side(tab, prob, vd, slots):
    return call(
        value_kernel,
        [shape((TOK, COLS))] * 4 + [shape((ROWS, COLS))],
        [SMEM, HBM, HBM, HBM],
        [HBM] * 5,
        [
            pltpu.VMEM((ITEMS, BLOCK, 2 * BLOCK), BF16),
            pltpu.VMEM((ROWS, COLS), BF16),
            pltpu.VMEM((ITEMS, BLOCK, HEAD_DIM), BF16),
            pltpu.VMEM((ROWS, COLS), BF16),
            pltpu.SemaphoreType.DMA((1,)),
            pltpu.SemaphoreType.DMA((ITEMS,)),
            pltpu.SemaphoreType.DMA((ITEMS,)),
            pltpu.SemaphoreType.DMA((TP + 1,)),
        ],
    )(tab, prob, vd, slots)


def query_kernel(
    tab, prob_ref, lse, kq_ref, vd_ref, slots1, slots2, att_ref,
    own, p1, p2, p3, stats_slots, stats,
    prob, k, vd, att, far_k, far_v, result, sems, k_sems, v_sems, prob_sems, out_sems, slot_sems,
):
    ctx = lax.axis_index("ctx")
    loads = [
        pltpu.make_async_copy(vd_ref, vd, sems.at[0]),
        pltpu.make_async_copy(att_ref, att, sems.at[1]),
        pltpu.make_async_copy(kq_ref.at[0], k, sems.at[2]),
    ]
    loads += far_copies(tab, slots2, far_v, v_sems)
    loads += far_copies(tab, slots1, far_k, k_sems)
    start_all(loads)
    start_probs(prob_ref, prob, prob_sems)
    wait_all(loads)
    fill_local(tab, far_v, vd.at[0])
    fill_local(tab, far_k, k)
    sublane = lax.broadcasted_iota(jnp.int32, (8, BLOCK), 0)

    def step(g, carry):
        cols = head_slice(g)
        for n in range(2):
            prob_copy(prob_ref, prob, n * GROUPS + g, prob_sems).wait()
        for n in range(2):
            rows = pl.ds(n * BLOCK, BLOCK)
            item = n * GROUPS + g
            do = vd[1, rows, cols]
            delta = jnp.sum(
                do.astype(F32) * att[rows, cols].astype(F32), axis=1, keepdims=True
            )
            p_own = prob[item, :, pl.ds(0, BLOCK)].astype(F32)
            p_far = prob[item, :, pl.ds(BLOCK, BLOCK)].astype(F32)
            ds_own = (p_own * (dot_t(do, vd[0, rows, cols]) - delta) * SCALE).astype(BF16)
            ds_far = (p_far * (dot_t(do, far_v[item]) - delta) * SCALE).astype(BF16)
            grad = dot(ds_own, k[rows, cols]) + dot(ds_far, far_k[item])
            result[rows, cols] = grad.astype(BF16)
            turned = jnp.transpose(jnp.broadcast_to(delta, (BLOCK, HEAD_DIM)))[0:8]
            stats[item] = jnp.where(sublane == 0, lse[item], turned)
        return carry

    lax.fori_loop(0, GROUPS, step, 0)
    copies = piece_copies(result, (own, p1, p2, p3), out_sems)
    for d in range(CTX):
        item = jnp.where(ctx > d, tab[0, d] * GROUPS + tab[1, d], 0)
        copies.append(pltpu.make_async_copy(stats.at[item], stats_slots.at[d], slot_sems.at[d]))
    run_copies(copies)


def query_side(tab, prob, lse, kq, vd, slots1, slots2, att):
    return call(
        query_kernel,
        [shape((TOK, COLS))] * 4 + [shape((CTX, 8, BLOCK), F32), shape((ITEMS, 8, BLOCK), F32)],
        [SMEM, HBM, VMEM] + [HBM] * 5,
        [HBM] * 5 + [VMEM],
        [
            pltpu.VMEM((ITEMS, BLOCK, 2 * BLOCK), BF16),
            pltpu.VMEM((ROWS, COLS), BF16),
            pltpu.VMEM((2, ROWS, COLS), BF16),
            pltpu.VMEM((ROWS, COLS), BF16),
            pltpu.VMEM((ITEMS, BLOCK, HEAD_DIM), BF16),
            pltpu.VMEM((ITEMS, BLOCK, HEAD_DIM), BF16),
            pltpu.VMEM((ROWS, COLS), BF16),
            pltpu.SemaphoreType.DMA((3,)),
            pltpu.SemaphoreType.DMA((ITEMS,)),
            pltpu.SemaphoreType.DMA((ITEMS,)),
            pltpu.SemaphoreType.DMA((ITEMS,)),
            pltpu.SemaphoreType.DMA((TP,)),
            pltpu.SemaphoreType.DMA((CTX,)),
        ],
    )(tab, prob, lse, kq, vd, slots1, slots2, att)


def key_terms(k, v, q, do, stats, causal):
    s = dot_t(k, q) * SCALE
    if causal is not None:
        s = jnp.where(causal, s, -jnp.inf)
    p = jnp.exp(s - stats[0:1])
    ds = (p * (dot_t(v, do) - stats[1:2]) * SCALE).astype(BF16)
    return dot(ds, q), dot(p.astype(BF16), do)


def near_kernel(tab, kq_ref, vd_ref, stats, gk_out, gv_out, kq, vd, gk, gv, sems, out_sems):
    run_copies(
        [
            pltpu.make_async_copy(kq_ref, kq, sems.at[0]),
            pltpu.make_async_copy(vd_ref, vd, sems.at[1]),
        ]
    )
    causal = lax.broadcasted_iota(jnp.int32, (BLOCK, BLOCK), 0) <= lax.broadcasted_iota(
        jnp.int32, (BLOCK, BLOCK), 1
    )

    def step(g, carry):
        cols = head_slice(g)
        for n in range(2):
            rows = pl.ds(n * BLOCK, BLOCK)
            gk[rows, cols], gv[rows, cols] = key_terms(
                kq[0, rows, cols], vd[0, rows, cols], kq[1, rows, cols], vd[1, rows, cols],
                stats[n * GROUPS + g], causal,
            )

        @pl.when(tab[3, GROUPS + g] == 2)
        def _():
            low, high = pl.ds(0, BLOCK), pl.ds(BLOCK, BLOCK)
            k_term, v_term = key_terms(
                kq[0, low, cols], vd[0, low, cols], kq[1, high, cols], vd[1, high, cols],
                stats[GROUPS + g], None,
            )
            gk[low, cols] += k_term
            gv[low, cols] += v_term

        return carry

    lax.fori_loop(0, GROUPS, step, 0)
    run_copies(
        [
            pltpu.make_async_copy(gk, gk_out, out_sems.at[0]),
            pltpu.make_async_copy(gv, gv_out, out_sems.at[1]),
        ]
    )


def near_side(tab, kq, vd, stats):
    return call(
        near_kernel,
        [shape((ROWS, COLS), F32)] * 2,
        [SMEM, HBM, HBM, VMEM],
        [HBM] * 2,
        [
            pltpu.VMEM((2, ROWS, COLS), BF16),
            pltpu.VMEM((2, ROWS, COLS), BF16),
            pltpu.VMEM((ROWS, COLS), F32),
            pltpu.VMEM((ROWS, COLS), F32),
            pltpu.SemaphoreType.DMA((2,)),
            pltpu.SemaphoreType.DMA((2,)),
        ],
    )(tab, kq, vd, stats)


def far_kernel(
    tab, kq_ref, vd_ref, slots1, slots2, stats, gk_ref, gv_ref,
    ko, k1, k2, k3, vo, v1, v2, v3,
    k, v, far_q, far_do, near, acc, result, sems, slot_sems, out_sems,
):
    ctx = lax.axis_index("ctx")

    def slot_copies(d):
        return [
            pltpu.make_async_copy(slots1.at[d], far_q.at[d], slot_sems.at[0, d]),
            pltpu.make_async_copy(slots2.at[d], far_do.at[d], slot_sems.at[1, d]),
        ]

    def start_slot(d, carry):
        start_all(slot_copies(d))
        return carry

    loads = [
        pltpu.make_async_copy(kq_ref.at[0], k, sems.at[0]),
        pltpu.make_async_copy(vd_ref.at[0], v, sems.at[1]),
    ]
    near_loads = [
        pltpu.make_async_copy(gk_ref, near.at[0], sems.at[2]),
        pltpu.make_async_copy(gv_ref, near.at[1], sems.at[3]),
    ]
    start_all(loads)
    pairs = (CTX - ctx) // 2
    lax.fori_loop(0, 2 * pairs, lambda j, c: start_slot((ctx + 1 + j) % CTX, c), 0)
    start_all(near_loads)
    acc[...] = jnp.zeros_like(acc)
    wait_all(loads)

    def step(pair, carry):
        picked = []
        for half in range(2):
            want = ctx + 1 + 2 * pair + half
            d = want % CTX
            wait_all(slot_copies(d))
            picked.append((d, (tab[2, d] == 1) & (want < CTX)))
        terms = []
        for d, filled in picked:
            rows, cols = block_slice(tab[0, d]), head_slice(tab[1, d])
            k_term, v_term = key_terms(
                k[rows, cols], v[rows, cols], far_q[d], far_do[d], stats[d], None
            )
            terms.append(
                (rows, cols, jnp.where(filled, k_term, 0.0), jnp.where(filled, v_term, 0.0))
            )
        for rows, cols, k_term, v_term in terms:
            acc[0, rows, cols] += k_term
            acc[1, rows, cols] += v_term
        return carry

    lax.fori_loop(0, pairs, step, 0)
    outs = ((ko, k1, k2, k3), (vo, v1, v2, v3))
    stores = []
    for which in range(2):
        near_loads[which].wait()
        result[which] = (near[which] + acc[which]).astype(BF16)
        copies = piece_copies(result.at[which], outs[which], out_sems.at[which])
        start_all(copies)
        stores += copies
    wait_all(stores)


def far_side(tab, kq, vd, slots1, slots2, stats, gk, gv):
    return call(
        far_kernel,
        [shape((TOK, COLS))] * 8,
        [SMEM] + [HBM] * 4 + [VMEM] + [HBM] * 2,
        [HBM] * 8,
        [
            pltpu.VMEM((ROWS, COLS), BF16),
            pltpu.VMEM((ROWS, COLS), BF16),
            pltpu.VMEM((CTX, BLOCK, HEAD_DIM), BF16),
            pltpu.VMEM((CTX, BLOCK, HEAD_DIM), BF16),
            pltpu.VMEM((2, ROWS, COLS), F32),
            pltpu.VMEM((2, ROWS, COLS), F32),
            pltpu.VMEM((2, ROWS, COLS), BF16),
            pltpu.SemaphoreType.DMA((4,)),
            pltpu.SemaphoreType.DMA((2, CTX)),
            pltpu.SemaphoreType.DMA((2, TP)),
        ],
    )(tab, kq, vd, slots1, slots2, stats, gk, gv)


def shards(queries, keys, values, dout, match):
    kq_in = exchange(cut(keys, queries))
    vd_in = exchange(cut(values, dout))
    tab = make_table(match)
    slots1, kq = pack(tab, keys, queries, kq_in)
    far1 = swap(slots1)
    slots2, vd = pack(tab, values, dout, vd_in)
    slots2, far1 = lax.optimization_barrier((slots2, far1))
    far2 = swap(slots2)
    prob, lse = prob_side(tab, kq, far1)
    *att, att_full = value_side(tab, prob, vd, far2)
    att_in = exchange(att[1:4])
    *gq, stats_slots, stats = query_side(tab, prob, lse, kq, vd, far1, far2, att_full)
    gq_in = exchange(gq[1:4])
    far_stats = swap(stats_slots)
    gk, gv = near_side(tab, kq, vd, stats)
    out = far_side(tab, kq, vd, far1, far2, far_stats, gk, gv)
    gk_in = exchange(out[1:4])
    gv_in = exchange(out[5:])
    return (join(att[0], att_in), join(gq[0], gq_in), join(out[0], gk_in), join(out[4], gv_in))


def solution(mesh):
    placed = P(("ctx", "tp"), None)
    return jax.shard_map(
        shards,
        mesh=mesh,
        in_specs=(placed, placed, placed, placed, P()),
        out_specs=(placed, placed, placed, placed),
        check_vma=False,
    )
```

```python
import jax
import jax.numpy as jnp
from jax import lax
from jax.experimental import pallas as pl
from jax.experimental.pallas import tpu as pltpu
from jax.sharding import PartitionSpec as P


HEAD_DIM = 128
BLOCK = 256
GROUPS = 10
CTX = 32
TP = 4
TOK = 128
ROWS = TP * TOK
COLS = GROUPS * HEAD_DIM
SCALE = HEAD_DIM ** (-0.5)
F32 = jnp.float32
BF16 = jnp.bfloat16


ANY = pl.BlockSpec(memory_space=pl.ANY)
SMEM = pl.BlockSpec(memory_space=pltpu.SMEM)
VMEM = pl.BlockSpec(memory_space=pltpu.VMEM)
HBM = pl.BlockSpec(memory_space=pltpu.HBM)


ITEMS = 2 * GROUPS
PARAMS = pltpu.CompilerParams(vmem_limit_bytes=40 * 1024 * 1024)


def shape(dims, dtype=BF16):
    return jax.ShapeDtypeStruct(dims, dtype)


def peer(step):
    return lax.rem(lax.axis_index("tp") + step, TP)


def col_slice(index):
    return pl.ds(pl.multiple_of(index * COLS, COLS), COLS)


def row_slice(index):
    return pl.ds(pl.multiple_of(index * TOK, TOK), TOK)


def block_slice(index):
    return pl.ds(pl.multiple_of(index * BLOCK, BLOCK), BLOCK)


def head_slice(index):
    return pl.ds(pl.multiple_of(index * HEAD_DIM, HEAD_DIM), HEAD_DIM)


def call(kernel, out_shape, in_specs, out_specs, scratch):
    many = isinstance(out_shape, list)
    outs = out_shape if many else [out_shape]
    specs = out_specs if many else [out_specs]
    outs = [
        pltpu.HBM(out.shape, out.dtype) if spec is HBM else out for out, spec in zip(outs, specs)
    ]

    def run(*operands):
        operands = [
            pltpu.with_memory_space_constraint(operand, pltpu.HBM) if spec is HBM else operand
            for operand, spec in zip(operands, in_specs)
        ]
        return pl.pallas_call(
            kernel,
            out_shape=outs if many else outs[0],
            in_specs=in_specs,
            out_specs=out_specs,
            scratch_shapes=scratch,
            compiler_params=PARAMS,
        )(*operands)

    return run


def run_copies(copies):
    for copy in copies:
        copy.start()
    for copy in copies:
        copy.wait()


def cut_kernel(a_ref, b_ref, p1, p2, p3, sems):
    copies = []
    for step, out in ((1, p1), (2, p2), (3, p3)):
        for which, ref in enumerate((a_ref, b_ref)):
            copies.append(
                pltpu.make_async_copy(
                    ref.at[:, col_slice(peer(step))], out.at[which], sems.at[len(copies)]
                )
            )
    run_copies(copies)


def cut(a, b):
    return call(
        cut_kernel,
        [shape((2, TOK, COLS))] * 3,
        [HBM] * 2,
        [VMEM] * 3,
        [pltpu.SemaphoreType.DMA((6,))],
    )(a, b)


def join_kernel(own, r1, r2, r3, out, sems):
    copies = []
    for step, ref in ((0, own), (1, r1), (2, r2), (3, r3)):
        copies.append(
            pltpu.make_async_copy(ref, out.at[:, col_slice(peer(TP - step))], sems.at[step])
        )
    run_copies(copies)


def join(own, received):
    return call(
        join_kernel, shape((TOK, TP * COLS)), [VMEM] * 4, HBM, [pltpu.SemaphoreType.DMA((4,))]
    )(own, *received)


def exchange(pieces):
    received = []
    for step, piece in zip((1, 2, 3), pieces):
        received.append(
            lax.ppermute(piece, "tp", [(i, (i + step) % TP) for i in range(TP)])
        )
    return tuple(received)


def gather_copies(a_ref, b_ref, received, held, sems, base):
    copies = []
    for which, ref in enumerate((a_ref, b_ref)):
        copies.append(
            pltpu.make_async_copy(
                ref.at[:, col_slice(peer(0))],
                held.at[which, row_slice(peer(0))],
                sems.at[base + len(copies)],
            )
        )
    for step, ref in zip((1, 2, 3), received):
        for which in range(2):
            copies.append(
                pltpu.make_async_copy(
                    ref.at[which],
                    held.at[which, row_slice(peer(TP - step))],
                    sems.at[base + len(copies)],
                )
            )
    return copies


def table_kernel(match, tab):
    ctx = lax.axis_index("ctx")

    def clear(d, carry):
        for row in range(5):
            tab[row, d] = 0
        return carry

    lax.fori_loop(0, CTX, clear, 0)

    def owner_side(d, carry):
        for n in range(2):
            for g in range(GROUPS):
                block = 2 * d + n
                m = match[g, block]

                @pl.when((m < block) & ((m >> 1) == ctx))
                def _():
                    tab[0, d] = m & 1
                    tab[1, d] = g
                    tab[2, d] = 1

        return carry

    lax.fori_loop(ctx + 1, CTX, owner_side, 0)
    for n in range(2):
        for g in range(GROUPS):
            block = 2 * ctx + n
            m = match[g, block]
            source = m >> 1
            item = n * GROUPS + g

            @pl.when((m < block) & (source != ctx))
            def _():
                tab[0, source] = n
                tab[1, source] = g
                tab[2, source] = 1
                tab[3, item] = 1
                tab[4, item] = source

            @pl.when((m < block) & (source == ctx))
            def _():
                tab[3, item] = 2


def make_table(match):
    return call(table_kernel, shape((8, CTX), jnp.int32), [SMEM], SMEM, [])(match)


def pack_kernel(tab, a_ref, b_ref, r1, r2, r3, out, held_out, held, sems, slot_sems):
    ctx = lax.axis_index("ctx")
    run_copies(gather_copies(a_ref, b_ref, (r1, r2, r3), held, sems, 0))
    copies = []
    for d in range(CTX):
        which = jnp.where(ctx > d, 1, 0)
        copies.append(
            pltpu.make_async_copy(
                held.at[which, block_slice(tab[0, d]), head_slice(tab[1, d])],
                out.at[d],
                slot_sems.at[d],
            )
        )
    copies.append(pltpu.make_async_copy(held, held_out, slot_sems.at[CTX]))
    run_copies(copies)


def pack(tab, a, b, received):
    return call(
        pack_kernel,
        [shape((CTX, BLOCK, HEAD_DIM)), shape((2, ROWS, COLS))],
        [SMEM] + [HBM] * 2 + [ANY] * 3,
        [HBM] * 2,
        [
            pltpu.VMEM((2, ROWS, COLS), BF16),
            pltpu.SemaphoreType.DMA((8,)),
            pltpu.SemaphoreType.DMA((CTX + 1,)),
        ],
    )(tab, a, b, *received)


def swap(slots):
    return lax.all_to_all(slots, "ctx", split_axis=0, concat_axis=0, tiled=True)


def dot(a, b):
    return lax.dot_general(a, b, (((1,), (0,)), ((), ())), preferred_element_type=F32)


def dot_t(a, b):
    return lax.dot_general(a, b, (((1,), (1,)), ((), ())), preferred_element_type=F32)


def dot_n(a, b):
    return lax.dot_general(a, b, (((0,), (0,)), ((), ())), preferred_element_type=F32)


STEP = 2
WIDE = STEP * HEAD_DIM
PAIR = pl.BlockSpec((2, ROWS, WIDE), lambda j, tab: (0, 0, j))
SECOND = pl.BlockSpec((1, ROWS, WIDE), lambda j, tab: (1, 0, j))
HEADS_ONE = pl.BlockSpec((ROWS, WIDE), lambda j, tab: (0, j))
PIECE = pl.BlockSpec((TOK, WIDE), lambda j, tab: (0, j))
PROBS = pl.BlockSpec((2, STEP, BLOCK, 2 * BLOCK), lambda j, tab: (0, j, 0, 0))
STATS = pl.BlockSpec((2, STEP, 8, BLOCK), lambda j, tab: (0, j, 0, 0))


def far_spec(n, u):
    return pl.BlockSpec(
        (1, BLOCK, HEAD_DIM), lambda j, tab: (tab[4, n * GROUPS + j * STEP + u], 0, 0)
    )


LANES = [(u, n) for u in range(STEP) for n in range(2)]
FAR = [far_spec(n, u) for u, n in LANES]
LOW, HIGH = pl.ds(0, BLOCK), pl.ds(BLOCK, BLOCK)


def lanes(j):
    for index, (u, n) in enumerate(LANES):
        yield index, u, n, j * STEP + u, pl.ds(n * BLOCK, BLOCK), pl.ds(u * HEAD_DIM, HEAD_DIM)


def by_group(kernel, out_shape, in_specs, out_specs, scratch, free=()):
    def run(tab, *operands):
        outs = [pltpu.HBM(out.shape, out.dtype) for out in out_shape]
        operands = [
            x if index in free else pltpu.with_memory_space_constraint(x, pltpu.HBM)
            for index, x in enumerate(operands)
        ]
        return pl.pallas_call(
            kernel,
            out_shape=outs,
            grid_spec=pltpu.PrefetchScalarGridSpec(
                num_scalar_prefetch=1,
                grid=(GROUPS // STEP,),
                in_specs=in_specs,
                out_specs=out_specs,
                scratch_shapes=scratch,
            ),
            compiler_params=PARAMS,
        )(tab, *operands)

    return run


def matched(tab, g, n, received, low):
    if n == 0:
        return received[0]
    return jnp.where(tab[3, GROUPS + g] == 2, low, received[0])


def prob_kernel(tab, kq, dout, *refs):
    far, (prob, lse_out, gv) = refs[: len(FAR)], refs[len(FAR) :]
    causal = lax.broadcasted_iota(jnp.int32, (BLOCK, BLOCK), 0) >= lax.broadcasted_iota(
        jnp.int32, (BLOCK, BLOCK), 1
    )
    for index, u, n, g, rows, cols in lanes(pl.program_id(0)):
        q = kq[1, rows, cols]
        kf = matched(tab, g, n, far[index], kq[0, LOW, cols])
        s_own = jnp.where(causal, dot_t(q, kq[0, rows, cols]) * SCALE, -jnp.inf)
        s_far = jnp.where(tab[3, n * GROUPS + g] > 0, dot_t(q, kf) * SCALE, -jnp.inf)
        top = jnp.maximum(
            jnp.max(s_own, axis=1, keepdims=True), jnp.max(s_far, axis=1, keepdims=True)
        )
        e_own = jnp.exp(s_own - top)
        e_far = jnp.exp(s_far - top)
        total = jnp.sum(e_own, axis=1, keepdims=True) + jnp.sum(e_far, axis=1, keepdims=True)
        inverse = 1.0 / total
        p_own = (e_own * inverse).astype(BF16)
        prob[n, u, :, LOW] = p_own
        prob[n, u, :, HIGH] = (e_far * inverse).astype(BF16)
        gv[rows, cols] = dot_n(p_own, dout[0, rows, cols])
        lse = jnp.broadcast_to(top + jnp.log(total), (BLOCK, HEAD_DIM))
        lse_out[n, u] = jnp.transpose(lse)[0:8]
    for index, u, n, g, rows, cols in lanes(pl.program_id(0)):
        if n == 1:

            @pl.when(tab[3, GROUPS + g] == 2)
            def _():
                gv[LOW, cols] += dot_n(prob[1, u, :, HIGH], dout[0, HIGH, cols])


def prob_side(tab, kq, vd, slots):
    return by_group(
        prob_kernel,
        [
            shape((2, GROUPS, BLOCK, 2 * BLOCK)),
            shape((2, GROUPS, 8, BLOCK), F32),
            shape((ROWS, COLS), F32),
        ],
        [PAIR, SECOND] + FAR,
        [PROBS, STATS, HEADS_ONE],
        [],
    )(tab, kq, vd, *[slots] * len(FAR))


def piece_copies(result, outs, sems):
    return [
        pltpu.make_async_copy(result.at[row_slice(peer(move))], out, sems.at[move])
        for move, out in enumerate(outs)
    ]


def start_all(copies):
    for copy in copies:
        copy.start()


def wait_all(copies):
    for copy in copies:
        copy.wait()


def value_kernel(tab, prob, lse, vd, *refs):
    far, (own, p1, p2, p3, full, stats_slots, stats, slot_sems) = (
        refs[: len(FAR)],
        refs[len(FAR) :],
    )
    j = pl.program_id(0)
    ctx = lax.axis_index("ctx")
    sublane = lax.broadcasted_iota(jnp.int32, (8, BLOCK), 0)
    for index, u, n, g, rows, cols in lanes(j):
        vf = matched(tab, g, n, far[index], vd[0, LOW, cols])
        att = dot(prob[n, u, :, LOW], vd[0, rows, cols]) + dot(prob[n, u, :, HIGH], vf)
        att = att.astype(BF16)
        full[rows, cols] = att
        delta = jnp.sum(vd[1, rows, cols].astype(F32) * att.astype(F32), axis=1, keepdims=True)
        turned = jnp.transpose(jnp.broadcast_to(delta, (BLOCK, HEAD_DIM)))[0:8]
        stats[n * GROUPS + g] = jnp.where(sublane == 0, lse[n, u], turned)
    for move, out in enumerate((own, p1, p2, p3)):
        out[...] = full[row_slice(peer(move))]

    @pl.when(j == GROUPS // STEP - 1)
    def _():
        copies = []
        for d in range(CTX):
            item = jnp.where(ctx > d, tab[0, d] * GROUPS + tab[1, d], 0)
            copies.append(
                pltpu.make_async_copy(stats.at[item], stats_slots.at[d], slot_sems.at[d])
            )
        run_copies(copies)


def value_side(tab, prob, lse, vd, slots):
    return by_group(
        value_kernel,
        [shape((TOK, COLS))] * 4 + [shape((ROWS, COLS)), shape((CTX, 8, BLOCK), F32)],
        [PROBS, STATS, PAIR] + FAR,
        [PIECE] * 4 + [HEADS_ONE, HBM],
        [pltpu.VMEM((ITEMS, 8, BLOCK), F32), pltpu.SemaphoreType.DMA((CTX,))],
        free=range(3, 3 + len(FAR)),
    )(tab, prob, lse, vd, *[slots] * len(FAR))


def query_kernel(tab, prob, kq, vd, att, *refs):
    count = len(FAR)
    far_k, far_v = refs[:count], refs[count : 2 * count]
    own, p1, p2, p3, gk, result, ds_last = refs[2 * count :]
    for index, u, n, g, rows, cols in lanes(pl.program_id(0)):
        do = vd[1, rows, cols]
        kf = matched(tab, g, n, far_k[index], kq[0, LOW, cols])
        vf = matched(tab, g, n, far_v[index], vd[0, LOW, cols])
        delta = jnp.sum(do.astype(F32) * att[rows, cols].astype(F32), axis=1, keepdims=True)
        p_own = prob[n, u, :, LOW].astype(F32)
        p_far = prob[n, u, :, HIGH].astype(F32)
        ds_own = (p_own * (dot_t(do, vd[0, rows, cols]) - delta) * SCALE).astype(BF16)
        ds_far = (p_far * (dot_t(do, vf) - delta) * SCALE).astype(BF16)
        result[rows, cols] = (dot(ds_own, kq[0, rows, cols]) + dot(ds_far, kf)).astype(BF16)
        gk[rows, cols] = dot_n(ds_own, kq[1, rows, cols])
        if n == 1:
            ds_last[u] = ds_far
    for move, out in enumerate((own, p1, p2, p3)):
        out[...] = result[row_slice(peer(move))]
    for index, u, n, g, rows, cols in lanes(pl.program_id(0)):
        if n == 1:

            @pl.when(tab[3, GROUPS + g] == 2)
            def _():
                gk[LOW, cols] += dot_n(ds_last[u], kq[1, HIGH, cols])


def query_side(tab, prob, kq, vd, att, slots1, slots2):
    return by_group(
        query_kernel,
        [shape((TOK, COLS))] * 4 + [shape((ROWS, COLS), F32)],
        [PROBS, PAIR, PAIR, HEADS_ONE] + FAR + FAR,
        [PIECE] * 4 + [HEADS_ONE],
        [pltpu.VMEM((ROWS, WIDE), BF16), pltpu.VMEM((STEP, BLOCK, BLOCK), BF16)],
    )(tab, prob, kq, vd, att, *[slots1] * len(FAR), *[slots2] * len(FAR))


def key_terms(k, v, q, do, stats):
    p = jnp.exp(dot_t(k, q) * SCALE - stats[0:1])
    ds = (p * (dot_t(v, do) - stats[1:2]) * SCALE).astype(BF16)
    return dot(ds, q), dot(p.astype(BF16), do)


def far_kernel(
    tab, kq_ref, vd_ref, slots1, slots2, stats, gk_ref, gv_ref,
    ko, k1, k2, k3, vo, v1, v2, v3,
    k, v, far_q, far_do, near, acc, result, sems, slot_sems, out_sems,
):
    ctx = lax.axis_index("ctx")

    def slot_copies(d):
        return [
            pltpu.make_async_copy(slots1.at[d], far_q.at[d], slot_sems.at[0, d]),
            pltpu.make_async_copy(slots2.at[d], far_do.at[d], slot_sems.at[1, d]),
        ]

    def start_slot(d, carry):
        start_all(slot_copies(d))
        return carry

    loads = [
        pltpu.make_async_copy(kq_ref.at[0], k, sems.at[0]),
        pltpu.make_async_copy(vd_ref.at[0], v, sems.at[1]),
    ]
    near_loads = [
        pltpu.make_async_copy(gk_ref, near.at[0], sems.at[2]),
        pltpu.make_async_copy(gv_ref, near.at[1], sems.at[3]),
    ]
    start_all(loads)
    pairs = (CTX - ctx) // 2
    lax.fori_loop(0, 2 * pairs, lambda j, c: start_slot((ctx + 1 + j) % CTX, c), 0)
    start_all(near_loads)
    acc[...] = jnp.zeros_like(acc)
    wait_all(loads)

    def step(pair, carry):
        picked = []
        for half in range(2):
            want = ctx + 1 + 2 * pair + half
            d = want % CTX
            wait_all(slot_copies(d))
            picked.append((d, (tab[2, d] == 1) & (want < CTX)))
        terms = []
        for d, filled in picked:
            rows, cols = block_slice(tab[0, d]), head_slice(tab[1, d])
            k_term, v_term = key_terms(
                k[rows, cols], v[rows, cols], far_q[d], far_do[d], stats[d]
            )
            terms.append(
                (rows, cols, jnp.where(filled, k_term, 0.0), jnp.where(filled, v_term, 0.0))
            )
        for rows, cols, k_term, v_term in terms:
            acc[0, rows, cols] += k_term
            acc[1, rows, cols] += v_term
        return carry

    lax.fori_loop(0, pairs, step, 0)
    outs = ((ko, k1, k2, k3), (vo, v1, v2, v3))
    stores = []
    for which in range(2):
        near_loads[which].wait()
        result[which] = (near[which] + acc[which]).astype(BF16)
        copies = piece_copies(result.at[which], outs[which], out_sems.at[which])
        start_all(copies)
        stores += copies
    wait_all(stores)


def far_side(tab, kq, vd, slots1, slots2, stats, gk, gv):
    return call(
        far_kernel,
        [shape((TOK, COLS))] * 8,
        [SMEM] + [HBM] * 4 + [VMEM] + [HBM] * 2,
        [HBM] * 8,
        [
            pltpu.VMEM((ROWS, COLS), BF16),
            pltpu.VMEM((ROWS, COLS), BF16),
            pltpu.VMEM((CTX, BLOCK, HEAD_DIM), BF16),
            pltpu.VMEM((CTX, BLOCK, HEAD_DIM), BF16),
            pltpu.VMEM((2, ROWS, COLS), F32),
            pltpu.VMEM((2, ROWS, COLS), F32),
            pltpu.VMEM((2, ROWS, COLS), BF16),
            pltpu.SemaphoreType.DMA((4,)),
            pltpu.SemaphoreType.DMA((2, CTX)),
            pltpu.SemaphoreType.DMA((2, TP)),
        ],
    )(tab, kq, vd, slots1, slots2, stats, gk, gv)


def shards(queries, keys, values, dout, match):
    kq_in = exchange(cut(keys, queries))
    vd_in = exchange(cut(values, dout))
    tab = make_table(match)
    slots1, kq = pack(tab, keys, queries, kq_in)
    far1 = swap(slots1)
    slots2, vd = pack(tab, values, dout, vd_in)
    slots2, far1 = lax.optimization_barrier((slots2, far1))
    far2 = swap(slots2)
    prob, lse, gv = prob_side(tab, kq, vd, far1)
    *att, att_full, stats_slots = value_side(tab, prob, lse, vd, far2)
    att_in = exchange(att[1:4])
    far_stats = swap(stats_slots)
    *gq, gk = query_side(tab, prob, kq, vd, att_full, far1, far2)
    gq_in = exchange(gq[1:4])
    out = far_side(tab, kq, vd, far1, far2, far_stats, gk, gv)
    gk_in = exchange(out[1:4])
    gv_in = exchange(out[5:])
    return (join(att[0], att_in), join(gq[0], gq_in), join(out[0], gk_in), join(out[4], gv_in))


def solution(mesh):
    placed = P(("ctx", "tp"), None)
    return jax.shard_map(
        shards,
        mesh=mesh,
        in_specs=(placed, placed, placed, placed, P()),
        out_specs=(placed, placed, placed, placed),
        check_vma=False,
    )
```

```python
import jax
import jax.numpy as jnp
from jax import lax
from jax.experimental import pallas as pl
from jax.experimental.pallas import tpu as pltpu
from jax.sharding import PartitionSpec as P


HEAD_DIM = 128
BLOCK = 256
GROUPS = 10
CTX = 32
TP = 4
TOK = 128
HALF = TOK // 2
ROWS = TP * TOK
COLS = GROUPS * HEAD_DIM
SCALE = HEAD_DIM ** (-0.5)
F32 = jnp.float32
BF16 = jnp.bfloat16


ANY = pl.BlockSpec(memory_space=pl.ANY)
SMEM = pl.BlockSpec(memory_space=pltpu.SMEM)
VMEM = pl.BlockSpec(memory_space=pltpu.VMEM)
HBM = pl.BlockSpec(memory_space=pltpu.HBM)


ITEMS = 2 * GROUPS
PARAMS = pltpu.CompilerParams(vmem_limit_bytes=40 * 1024 * 1024)


def shape(dims, dtype=BF16):
    return jax.ShapeDtypeStruct(dims, dtype)


def peer(step):
    return lax.rem(lax.axis_index("tp") + step, TP)


def col_slice(index):
    return pl.ds(pl.multiple_of(index * COLS, COLS), COLS)


def row_slice(index):
    return pl.ds(pl.multiple_of(index * TOK, TOK), TOK)


def block_slice(index):
    return pl.ds(pl.multiple_of(index * BLOCK, BLOCK), BLOCK)


def head_slice(index):
    return pl.ds(pl.multiple_of(index * HEAD_DIM, HEAD_DIM), HEAD_DIM)


def call(kernel, out_shape, in_specs, out_specs, scratch):
    many = isinstance(out_shape, list)
    outs = out_shape if many else [out_shape]
    specs = out_specs if many else [out_specs]
    outs = [
        pltpu.HBM(out.shape, out.dtype) if spec is HBM else out for out, spec in zip(outs, specs)
    ]

    def run(*operands):
        operands = [
            pltpu.with_memory_space_constraint(operand, pltpu.HBM) if spec is HBM else operand
            for operand, spec in zip(operands, in_specs)
        ]
        return pl.pallas_call(
            kernel,
            out_shape=outs if many else outs[0],
            in_specs=in_specs,
            out_specs=out_specs,
            scratch_shapes=scratch,
            compiler_params=PARAMS,
        )(*operands)

    return run


def run_copies(copies):
    for copy in copies:
        copy.start()
    for copy in copies:
        copy.wait()


def cut(a, b, base, size):
    def kernel(a_ref, b_ref, p1, p2, p3, sems):
        copies = []
        for step, out in ((1, p1), (2, p2), (3, p3)):
            for which, ref in enumerate((a_ref, b_ref)):
                copies.append(
                    pltpu.make_async_copy(
                        ref.at[pl.ds(base, size), col_slice(peer(step))],
                        out.at[which],
                        sems.at[len(copies)],
                    )
                )
        run_copies(copies)

    return call(
        kernel, [shape((2, size, COLS))] * 3, [HBM] * 2, [VMEM] * 3, [pltpu.SemaphoreType.DMA((6,))]
    )(a, b)


def join_kernel(own, r1, r2, r3, out, sems):
    copies = []
    for step, ref in ((0, own), (1, r1), (2, r2), (3, r3)):
        copies.append(
            pltpu.make_async_copy(ref, out.at[:, col_slice(peer(TP - step))], sems.at[step])
        )
    run_copies(copies)


def join(own, received):
    return call(
        join_kernel, shape((TOK, TP * COLS)), [VMEM] * 4, HBM, [pltpu.SemaphoreType.DMA((4,))]
    )(own, *received)


def exchange(pieces):
    received = []
    for step, piece in zip((1, 2, 3), pieces):
        received.append(
            lax.ppermute(piece, "tp", [(i, (i + step) % TP) for i in range(TP)])
        )
    return tuple(received)


def gather_copies(a_ref, b_ref, received, held, sems, base, size, at, stride):
    def place(index):
        start = pl.multiple_of(index * stride + at, size)
        return pl.ds(start, size)

    copies = []
    for which, ref in enumerate((a_ref, b_ref)):
        copies.append(
            pltpu.make_async_copy(
                ref.at[pl.ds(base, size), col_slice(peer(0))],
                held.at[which, place(peer(0))],
                sems.at[len(copies)],
            )
        )
    for step, ref in zip((1, 2, 3), received):
        for which in range(2):
            copies.append(
                pltpu.make_async_copy(
                    ref.at[which], held.at[which, place(peer(TP - step))], sems.at[len(copies)]
                )
            )
    return copies


def table_kernel(match, tab):
    ctx = lax.axis_index("ctx")

    def clear(d, carry):
        for row in range(5):
            tab[row, d] = 0
        return carry

    lax.fori_loop(0, CTX, clear, 0)

    def owner_side(d, carry):
        for n in range(2):
            for g in range(GROUPS):
                block = 2 * d + n
                m = match[g, block]

                @pl.when((m < block) & ((m >> 1) == ctx))
                def _():
                    tab[0, d] = m & 1
                    tab[1, d] = g
                    tab[2, d] = 1

        return carry

    lax.fori_loop(ctx + 1, CTX, owner_side, 0)
    for n in range(2):
        for g in range(GROUPS):
            block = 2 * ctx + n
            m = match[g, block]
            source = m >> 1
            item = n * GROUPS + g

            @pl.when((m < block) & (source != ctx))
            def _():
                tab[0, source] = n
                tab[1, source] = g
                tab[2, source] = 1
                tab[3, item] = 1
                tab[4, item] = source

            @pl.when((m < block) & (source == ctx))
            def _():
                tab[3, item] = 2


def make_table(match):
    return call(table_kernel, shape((8, CTX), jnp.int32), [SMEM], SMEM, [])(match)


def pack(tab, a, b, received, base, size):
    def kernel(tab, a_ref, b_ref, r1, r2, r3, out, held_out, held, sems, slot_sems):
        ctx = lax.axis_index("ctx")
        run_copies(gather_copies(a_ref, b_ref, (r1, r2, r3), held, sems, base, size, 0, size))
        copies = []
        for d in range(CTX):
            which = jnp.where(ctx > d, 1, 0)
            rows = pl.ds(pl.multiple_of(tab[0, d] * 2 * size, 2 * size), 2 * size)
            copies.append(
                pltpu.make_async_copy(
                    held.at[which, rows, head_slice(tab[1, d])], out.at[d], slot_sems.at[d]
                )
            )
        copies.append(pltpu.make_async_copy(held, held_out, slot_sems.at[CTX]))
        run_copies(copies)

    return call(
        kernel,
        [shape((CTX, 2 * size, HEAD_DIM)), shape((2, TP * size, COLS))],
        [SMEM] + [HBM] * 2 + [ANY] * 3,
        [HBM] * 2,
        [
            pltpu.VMEM((2, TP * size, COLS), BF16),
            pltpu.SemaphoreType.DMA((8,)),
            pltpu.SemaphoreType.DMA((CTX + 1,)),
        ],
    )(tab, a, b, *received)


def hold_kernel(a_ref, b_ref, out, held, sems, out_sem):
    copies = []
    for part, ref in enumerate((a_ref, b_ref)):
        for index in range(TP):
            copies.append(
                pltpu.make_async_copy(
                    ref.at[:, pl.ds(index * HALF, HALF)],
                    held.at[:, pl.ds(index * TOK + part * HALF, HALF)],
                    sems.at[len(copies)],
                )
            )
    run_copies(copies)
    run_copies([pltpu.make_async_copy(held, out, out_sem.at[0])])


def hold(a, b):
    return call(
        hold_kernel,
        shape((2, ROWS, COLS)),
        [HBM] * 2,
        HBM,
        [
            pltpu.VMEM((2, ROWS, COLS), BF16),
            pltpu.SemaphoreType.DMA((2 * TP,)),
            pltpu.SemaphoreType.DMA((1,)),
        ],
    )(a, b)


def swap(slots):
    return lax.all_to_all(slots, "ctx", split_axis=0, concat_axis=0, tiled=True)


def dot(a, b):
    return lax.dot_general(a, b, (((1,), (0,)), ((), ())), preferred_element_type=F32)


def dot_t(a, b):
    return lax.dot_general(a, b, (((1,), (1,)), ((), ())), preferred_element_type=F32)


def dot_n(a, b):
    return lax.dot_general(a, b, (((0,), (0,)), ((), ())), preferred_element_type=F32)


STEP = 2
WIDE = STEP * HEAD_DIM
PAIR = pl.BlockSpec((2, ROWS, WIDE), lambda j, tab: (0, 0, j))
SECOND = pl.BlockSpec((1, ROWS, WIDE), lambda j, tab: (1, 0, j))
HEADS_ONE = pl.BlockSpec((ROWS, WIDE), lambda j, tab: (0, j))
PIECE = pl.BlockSpec((TOK, WIDE), lambda j, tab: (0, j))
PROBS = pl.BlockSpec((2, STEP, BLOCK, 2 * BLOCK), lambda j, tab: (0, j, 0, 0))
STATS = pl.BlockSpec((2, STEP, 8, BLOCK), lambda j, tab: (0, j, 0, 0))


def far_spec(n, u):
    return pl.BlockSpec(
        (1, BLOCK, HEAD_DIM), lambda j, tab: (tab[4, n * GROUPS + j * STEP + u], 0, 0)
    )


def half_spec(n, u):
    return pl.BlockSpec(
        (1, 2, HALF, HEAD_DIM), lambda j, tab: (tab[4, n * GROUPS + j * STEP + u], 0, 0, 0)
    )


def woven(first, second):
    return jnp.concatenate([first[0, 0], second[0, 0], first[0, 1], second[0, 1]], axis=0)


LANES = [(u, n) for u in range(STEP) for n in range(2)]
FAR = [far_spec(n, u) for u, n in LANES]
HALVES = [half_spec(n, u) for u, n in LANES]
LOW, HIGH = pl.ds(0, BLOCK), pl.ds(BLOCK, BLOCK)


def lanes(j):
    for index, (u, n) in enumerate(LANES):
        yield index, u, n, j * STEP + u, pl.ds(n * BLOCK, BLOCK), pl.ds(u * HEAD_DIM, HEAD_DIM)


def by_group(kernel, out_shape, in_specs, out_specs, scratch, free=()):
    def run(tab, *operands):
        outs = [pltpu.HBM(out.shape, out.dtype) for out in out_shape]
        operands = [
            x if index in free else pltpu.with_memory_space_constraint(x, pltpu.HBM)
            for index, x in enumerate(operands)
        ]
        return pl.pallas_call(
            kernel,
            out_shape=outs,
            grid_spec=pltpu.PrefetchScalarGridSpec(
                num_scalar_prefetch=1,
                grid=(GROUPS // STEP,),
                in_specs=in_specs,
                out_specs=out_specs,
                scratch_shapes=scratch,
            ),
            compiler_params=PARAMS,
        )(tab, *operands)

    return run


def matched(tab, g, n, received, low):
    if n == 0:
        return received
    return jnp.where(tab[3, GROUPS + g] == 2, low, received)


def prob_kernel(tab, kq, dout, *refs):
    count = len(FAR)
    first, second, (prob, lse_out, gv) = refs[:count], refs[count : 2 * count], refs[2 * count :]
    causal = lax.broadcasted_iota(jnp.int32, (BLOCK, BLOCK), 0) >= lax.broadcasted_iota(
        jnp.int32, (BLOCK, BLOCK), 1
    )
    for index, u, n, g, rows, cols in lanes(pl.program_id(0)):
        q = kq[1, rows, cols]
        kf = matched(tab, g, n, woven(first[index], second[index]), kq[0, LOW, cols])
        s_own = jnp.where(causal, dot_t(q, kq[0, rows, cols]) * SCALE, -jnp.inf)
        s_far = jnp.where(tab[3, n * GROUPS + g] > 0, dot_t(q, kf) * SCALE, -jnp.inf)
        top = jnp.maximum(
            jnp.max(s_own, axis=1, keepdims=True), jnp.max(s_far, axis=1, keepdims=True)
        )
        e_own = jnp.exp(s_own - top)
        e_far = jnp.exp(s_far - top)
        total = jnp.sum(e_own, axis=1, keepdims=True) + jnp.sum(e_far, axis=1, keepdims=True)
        inverse = 1.0 / total
        p_own = (e_own * inverse).astype(BF16)
        prob[n, u, :, LOW] = p_own
        prob[n, u, :, HIGH] = (e_far * inverse).astype(BF16)
        gv[rows, cols] = dot_n(p_own, dout[0, rows, cols])
        lse = jnp.broadcast_to(top + jnp.log(total), (BLOCK, HEAD_DIM))
        lse_out[n, u] = jnp.transpose(lse)[0:8]
    for index, u, n, g, rows, cols in lanes(pl.program_id(0)):
        if n == 1:

            @pl.when(tab[3, GROUPS + g] == 2)
            def _():
                gv[LOW, cols] += dot_n(prob[1, u, :, HIGH], dout[0, HIGH, cols])


def prob_side(tab, kq, vd, slots_a, slots_b):
    return by_group(
        prob_kernel,
        [
            shape((2, GROUPS, BLOCK, 2 * BLOCK)),
            shape((2, GROUPS, 8, BLOCK), F32),
            shape((ROWS, COLS), F32),
        ],
        [PAIR, SECOND] + HALVES * 2,
        [PROBS, STATS, HEADS_ONE],
        [],
    )(tab, kq, vd, *[slots_a] * len(FAR), *[slots_b] * len(FAR))


def piece_copies(result, outs, sems):
    return [
        pltpu.make_async_copy(result.at[row_slice(peer(move))], out, sems.at[move])
        for move, out in enumerate(outs)
    ]


def start_all(copies):
    for copy in copies:
        copy.start()


def wait_all(copies):
    for copy in copies:
        copy.wait()


def value_kernel(tab, prob, lse, vd, *refs):
    far, (own, p1, p2, p3, full, stats_slots, stats, slot_sems) = (
        refs[: len(FAR)],
        refs[len(FAR) :],
    )
    j = pl.program_id(0)
    ctx = lax.axis_index("ctx")
    sublane = lax.broadcasted_iota(jnp.int32, (8, BLOCK), 0)
    for index, u, n, g, rows, cols in lanes(j):
        vf = matched(tab, g, n, far[index][0], vd[0, LOW, cols])
        att = dot(prob[n, u, :, LOW], vd[0, rows, cols]) + dot(prob[n, u, :, HIGH], vf)
        att = att.astype(BF16)
        full[rows, cols] = att
        delta = jnp.sum(vd[1, rows, cols].astype(F32) * att.astype(F32), axis=1, keepdims=True)
        turned = jnp.transpose(jnp.broadcast_to(delta, (BLOCK, HEAD_DIM)))[0:8]
        stats[n * GROUPS + g] = jnp.where(sublane == 0, lse[n, u], turned)
    for move, out in enumerate((own, p1, p2, p3)):
        out[...] = full[row_slice(peer(move))]

    @pl.when(j == GROUPS // STEP - 1)
    def _():
        copies = []
        for d in range(CTX):
            item = jnp.where(ctx > d, tab[0, d] * GROUPS + tab[1, d], 0)
            copies.append(
                pltpu.make_async_copy(stats.at[item], stats_slots.at[d], slot_sems.at[d])
            )
        run_copies(copies)


def value_side(tab, prob, lse, vd, slots):
    return by_group(
        value_kernel,
        [shape((TOK, COLS))] * 4 + [shape((ROWS, COLS)), shape((CTX, 8, BLOCK), F32)],
        [PROBS, STATS, PAIR] + FAR,
        [PIECE] * 4 + [HEADS_ONE, HBM],
        [pltpu.VMEM((ITEMS, 8, BLOCK), F32), pltpu.SemaphoreType.DMA((CTX,))],
        free=range(3, 3 + len(FAR)),
    )(tab, prob, lse, vd, *[slots] * len(FAR))


def query_kernel(tab, prob, kq, vd, att, *refs):
    count = len(FAR)
    first, second, far_v = refs[:count], refs[count : 2 * count], refs[2 * count : 3 * count]
    own, p1, p2, p3, gk, result, ds_last = refs[3 * count :]
    for index, u, n, g, rows, cols in lanes(pl.program_id(0)):
        do = vd[1, rows, cols]
        kf = matched(tab, g, n, woven(first[index], second[index]), kq[0, LOW, cols])
        vf = matched(tab, g, n, far_v[index][0], vd[0, LOW, cols])
        delta = jnp.sum(do.astype(F32) * att[rows, cols].astype(F32), axis=1, keepdims=True)
        p_own = prob[n, u, :, LOW].astype(F32)
        p_far = prob[n, u, :, HIGH].astype(F32)
        ds_own = (p_own * (dot_t(do, vd[0, rows, cols]) - delta) * SCALE).astype(BF16)
        ds_far = (p_far * (dot_t(do, vf) - delta) * SCALE).astype(BF16)
        result[rows, cols] = (dot(ds_own, kq[0, rows, cols]) + dot(ds_far, kf)).astype(BF16)
        gk[rows, cols] = dot_n(ds_own, kq[1, rows, cols])
        if n == 1:
            ds_last[u] = ds_far
    for move, out in enumerate((own, p1, p2, p3)):
        out[...] = result[row_slice(peer(move))]
    for index, u, n, g, rows, cols in lanes(pl.program_id(0)):
        if n == 1:

            @pl.when(tab[3, GROUPS + g] == 2)
            def _():
                gk[LOW, cols] += dot_n(ds_last[u], kq[1, HIGH, cols])


def query_side(tab, prob, kq, vd, att, slots_a, slots_b, slots2):
    return by_group(
        query_kernel,
        [shape((TOK, COLS))] * 4 + [shape((ROWS, COLS), F32)],
        [PROBS, PAIR, PAIR, HEADS_ONE] + HALVES * 2 + FAR,
        [PIECE] * 4 + [HEADS_ONE],
        [pltpu.VMEM((ROWS, WIDE), BF16), pltpu.VMEM((STEP, BLOCK, BLOCK), BF16)],
    )(
        tab, prob, kq, vd, att,
        *[slots_a] * len(FAR), *[slots_b] * len(FAR), *[slots2] * len(FAR),
    )


def key_terms(k, v, q, do, stats):
    p = jnp.exp(dot_t(k, q) * SCALE - stats[0:1])
    ds = (p * (dot_t(v, do) - stats[1:2]) * SCALE).astype(BF16)
    return dot(ds, q), dot(p.astype(BF16), do)


JOBS = 4


def far_kernel(
    tab, kq_ref, vd_ref, slots_a, slots_b, slots2, stats, gk_ref, gv_ref,
    ko, k1, k2, k3, vo, v1, v2, v3,
    k, v, far_q, far_do, near, acc, result, sems, slot_sems, out_sems,
):
    ctx = lax.axis_index("ctx")

    def slot_copies(d):
        return [
            pltpu.make_async_copy(slots_a.at[d], far_q.at[d, :, 0], slot_sems.at[0, d]),
            pltpu.make_async_copy(slots_b.at[d], far_q.at[d, :, 1], slot_sems.at[1, d]),
            pltpu.make_async_copy(slots2.at[d], far_do.at[d], slot_sems.at[2, d]),
        ]

    def start_slot(d, carry):
        start_all(slot_copies(d))
        return carry

    loads = [
        pltpu.make_async_copy(kq_ref.at[0], k, sems.at[0]),
        pltpu.make_async_copy(vd_ref.at[0], v, sems.at[1]),
    ]
    near_loads = [
        pltpu.make_async_copy(gk_ref, near.at[0], sems.at[2]),
        pltpu.make_async_copy(gv_ref, near.at[1], sems.at[3]),
    ]
    start_all(loads)
    rounds = (CTX - 1 - ctx + JOBS - 1) // JOBS
    lax.fori_loop(0, JOBS * rounds, lambda j, c: start_slot((ctx + 1 + j) % CTX, c), 0)
    start_all(near_loads)
    acc[...] = jnp.zeros_like(acc)
    wait_all(loads)

    def step(turn, carry):
        picked = []
        for job in range(JOBS):
            want = ctx + 1 + JOBS * turn + job
            d = want % CTX
            wait_all(slot_copies(d))
            picked.append((d, (tab[2, d] == 1) & (want < CTX)))
        terms = []
        for d, filled in picked:
            rows, cols = block_slice(tab[0, d]), head_slice(tab[1, d])
            k_term, v_term = key_terms(
                k[rows, cols], v[rows, cols], far_q[d].reshape(BLOCK, HEAD_DIM), far_do[d], stats[d]
            )
            terms.append(
                (rows, cols, jnp.where(filled, k_term, 0.0), jnp.where(filled, v_term, 0.0))
            )
        for rows, cols, k_term, v_term in terms:
            acc[0, rows, cols] += k_term
            acc[1, rows, cols] += v_term
        return carry

    lax.fori_loop(0, rounds, step, 0)
    outs = ((ko, k1, k2, k3), (vo, v1, v2, v3))
    stores = []
    for which in range(2):
        near_loads[which].wait()
        result[which] = (near[which] + acc[which]).astype(BF16)
        copies = piece_copies(result.at[which], outs[which], out_sems.at[which])
        start_all(copies)
        stores += copies
    wait_all(stores)


def far_side(tab, kq, vd, slots_a, slots_b, slots2, stats, gk, gv):
    return call(
        far_kernel,
        [shape((TOK, COLS))] * 8,
        [SMEM] + [HBM] * 5 + [VMEM] + [HBM] * 2,
        [HBM] * 8,
        [
            pltpu.VMEM((ROWS, COLS), BF16),
            pltpu.VMEM((ROWS, COLS), BF16),
            pltpu.VMEM((CTX, 2, 2, HALF, HEAD_DIM), BF16),
            pltpu.VMEM((CTX, BLOCK, HEAD_DIM), BF16),
            pltpu.VMEM((2, ROWS, COLS), F32),
            pltpu.VMEM((2, ROWS, COLS), F32),
            pltpu.VMEM((2, ROWS, COLS), BF16),
            pltpu.SemaphoreType.DMA((4,)),
            pltpu.SemaphoreType.DMA((3, CTX)),
            pltpu.SemaphoreType.DMA((2, TP)),
        ],
    )(tab, kq, vd, slots_a, slots_b, slots2, stats, gk, gv)


def shards(queries, keys, values, dout, match):
    ka_in = exchange(cut(keys, queries, 0, HALF))
    kb_in = exchange(cut(keys, queries, HALF, HALF))
    vd_in = exchange(cut(values, dout, 0, TOK))
    tab = make_table(match)
    slots_a, held_a = pack(tab, keys, queries, ka_in, 0, HALF)
    far_a = swap(slots_a)
    slots_b, held_b = pack(tab, keys, queries, kb_in, HALF, HALF)
    slots_b, far_a = lax.optimization_barrier((slots_b, far_a))
    far_b = swap(slots_b)
    slots2, vd = pack(tab, values, dout, vd_in, 0, TOK)
    slots2, far_b = lax.optimization_barrier((slots2, far_b))
    far2 = swap(slots2)
    kq = hold(held_a, held_b)
    far_a = far_a.reshape(CTX, 2, HALF, HEAD_DIM)
    far_b = far_b.reshape(CTX, 2, HALF, HEAD_DIM)
    prob, lse, gv = prob_side(tab, kq, vd, far_a, far_b)
    *att, att_full, stats_slots = value_side(tab, prob, lse, vd, far2)
    att_in = exchange(att[1:4])
    far_stats = swap(stats_slots)
    *gq, gk = query_side(tab, prob, kq, vd, att_full, far_a, far_b, far2)
    gq_in = exchange(gq[1:4])
    out = far_side(tab, kq, vd, far_a, far_b, far2, far_stats, gk, gv)
    gk_in = exchange(out[1:4])
    gv_in = exchange(out[5:])
    return (join(att[0], att_in), join(gq[0], gq_in), join(out[0], gk_in), join(out[4], gv_in))


def solution(mesh):
    placed = P(("ctx", "tp"), None)
    return jax.shard_map(
        shards,
        mesh=mesh,
        in_specs=(placed, placed, placed, placed, P()),
        out_specs=(placed, placed, placed, placed),
        check_vma=False,
    )
```

```python
import jax
import jax.numpy as jnp
from jax import lax
from jax.experimental import pallas as pl
from jax.experimental.pallas import tpu as pltpu
from jax.sharding import PartitionSpec as P


HEAD_DIM = 128
BLOCK = 256
GROUPS = 10
CTX = 32
TP = 4
TOK = 128
HALF = TOK // 2
ROWS = TP * TOK
COLS = GROUPS * HEAD_DIM
SCALE = HEAD_DIM ** (-0.5)
F32 = jnp.float32
BF16 = jnp.bfloat16


ANY = pl.BlockSpec(memory_space=pl.ANY)
SMEM = pl.BlockSpec(memory_space=pltpu.SMEM)
VMEM = pl.BlockSpec(memory_space=pltpu.VMEM)
HBM = pl.BlockSpec(memory_space=pltpu.HBM)


ITEMS = 2 * GROUPS
PARAMS = pltpu.CompilerParams(vmem_limit_bytes=40 * 1024 * 1024)


def shape(dims, dtype=BF16):
    return jax.ShapeDtypeStruct(dims, dtype)


def peer(step):
    return lax.rem(lax.axis_index("tp") + step, TP)


def col_slice(index):
    return pl.ds(pl.multiple_of(index * COLS, COLS), COLS)


def row_slice(index):
    return pl.ds(pl.multiple_of(index * TOK, TOK), TOK)


def block_slice(index):
    return pl.ds(pl.multiple_of(index * BLOCK, BLOCK), BLOCK)


def head_slice(index):
    return pl.ds(pl.multiple_of(index * HEAD_DIM, HEAD_DIM), HEAD_DIM)


def call(kernel, out_shape, in_specs, out_specs, scratch):
    many = isinstance(out_shape, list)
    outs = out_shape if many else [out_shape]
    specs = out_specs if many else [out_specs]
    outs = [
        pltpu.HBM(out.shape, out.dtype) if spec is HBM else out for out, spec in zip(outs, specs)
    ]

    def run(*operands):
        operands = [
            pltpu.with_memory_space_constraint(operand, pltpu.HBM) if spec is HBM else operand
            for operand, spec in zip(operands, in_specs)
        ]
        return pl.pallas_call(
            kernel,
            out_shape=outs if many else outs[0],
            in_specs=in_specs,
            out_specs=out_specs,
            scratch_shapes=scratch,
            compiler_params=PARAMS,
        )(*operands)

    return run


def run_copies(copies):
    for copy in copies:
        copy.start()
    for copy in copies:
        copy.wait()


def cut(a, b, base, size):
    def kernel(a_ref, b_ref, p1, p2, p3, sems):
        copies = []
        for step, out in ((1, p1), (2, p2), (3, p3)):
            for which, ref in enumerate((a_ref, b_ref)):
                copies.append(
                    pltpu.make_async_copy(
                        ref.at[pl.ds(base, size), col_slice(peer(step))],
                        out.at[which],
                        sems.at[len(copies)],
                    )
                )
        run_copies(copies)

    return call(
        kernel, [shape((2, size, COLS))] * 3, [HBM] * 2, [VMEM] * 3, [pltpu.SemaphoreType.DMA((6,))]
    )(a, b)


def join_kernel(own, r1, r2, r3, out, sems):
    copies = []
    for step, ref in ((0, own), (1, r1), (2, r2), (3, r3)):
        copies.append(
            pltpu.make_async_copy(ref, out.at[:, col_slice(peer(TP - step))], sems.at[step])
        )
    run_copies(copies)


def join(own, received):
    return call(
        join_kernel, shape((TOK, TP * COLS)), [VMEM] * 4, HBM, [pltpu.SemaphoreType.DMA((4,))]
    )(own, *received)


def exchange(pieces):
    received = []
    for step, piece in zip((1, 2, 3), pieces):
        received.append(
            lax.ppermute(piece, "tp", [(i, (i + step) % TP) for i in range(TP)])
        )
    return tuple(received)


def gather_copies(a_ref, b_ref, received, held, sems, base, size, at, stride):
    def place(index):
        start = pl.multiple_of(index * stride + at, size)
        return pl.ds(start, size)

    copies = []
    for which, ref in enumerate((a_ref, b_ref)):
        copies.append(
            pltpu.make_async_copy(
                ref.at[pl.ds(base, size), col_slice(peer(0))],
                held.at[which, place(peer(0))],
                sems.at[len(copies)],
            )
        )
    for step, ref in zip((1, 2, 3), received):
        for which in range(2):
            copies.append(
                pltpu.make_async_copy(
                    ref.at[which], held.at[which, place(peer(TP - step))], sems.at[len(copies)]
                )
            )
    return copies


def table_kernel(match, tab):
    ctx = lax.axis_index("ctx")

    def clear(d, carry):
        for row in range(5):
            tab[row, d] = 0
        return carry

    lax.fori_loop(0, CTX, clear, 0)

    def owner_side(d, carry):
        code = jnp.int32(0)
        for n in range(2):
            for g in range(GROUPS):
                block = 2 * d + n
                m = match[g, block]
                hit = (m < block) & ((m >> 1) == ctx)
                code = jnp.where(hit, 32 + g + 16 * (m & 1), code)
        tab[0, d] = (code >> 4) & 1
        tab[1, d] = code & 15
        tab[2, d] = code >> 5
        return carry

    lax.fori_loop(ctx + 1, CTX, owner_side, 0)
    for n in range(2):
        for g in range(GROUPS):
            block = 2 * ctx + n
            m = match[g, block]
            source = m >> 1
            item = n * GROUPS + g

            @pl.when((m < block) & (source != ctx))
            def _():
                tab[0, source] = n
                tab[1, source] = g
                tab[2, source] = 1
                tab[3, item] = 1
                tab[4, item] = source

            @pl.when((m < block) & (source == ctx))
            def _():
                tab[3, item] = 2


def make_table(match):
    return call(table_kernel, shape((8, CTX), jnp.int32), [SMEM], SMEM, [])(match)


def pack(tab, a, b, received, base, size):
    def kernel(tab, a_ref, b_ref, r1, r2, r3, out, held_out, held, sems, slot_sems):
        ctx = lax.axis_index("ctx")
        run_copies(gather_copies(a_ref, b_ref, (r1, r2, r3), held, sems, base, size, 0, size))
        copies = []
        for d in range(CTX):
            which = jnp.where(ctx > d, 1, 0)
            rows = pl.ds(pl.multiple_of(tab[0, d] * 2 * size, 2 * size), 2 * size)
            copies.append(
                pltpu.make_async_copy(
                    held.at[which, rows, head_slice(tab[1, d])], out.at[d], slot_sems.at[d]
                )
            )
        copies.append(pltpu.make_async_copy(held, held_out, slot_sems.at[CTX]))
        run_copies(copies)

    return call(
        kernel,
        [shape((CTX, 2 * size, HEAD_DIM)), shape((2, TP * size, COLS))],
        [SMEM] + [HBM] * 2 + [ANY] * 3,
        [HBM] * 2,
        [
            pltpu.VMEM((2, TP * size, COLS), BF16),
            pltpu.SemaphoreType.DMA((8,)),
            pltpu.SemaphoreType.DMA((CTX + 1,)),
        ],
    )(tab, a, b, *received)


def hold_kernel(a_ref, b_ref, out, held, sems, out_sem):
    copies = []
    for part, ref in enumerate((a_ref, b_ref)):
        for index in range(TP):
            copies.append(
                pltpu.make_async_copy(
                    ref.at[:, pl.ds(index * HALF, HALF)],
                    held.at[:, pl.ds(index * TOK + part * HALF, HALF)],
                    sems.at[len(copies)],
                )
            )
    run_copies(copies)
    run_copies([pltpu.make_async_copy(held, out, out_sem.at[0])])


def hold(a, b):
    return call(
        hold_kernel,
        shape((2, ROWS, COLS)),
        [HBM] * 2,
        HBM,
        [
            pltpu.VMEM((2, ROWS, COLS), BF16),
            pltpu.SemaphoreType.DMA((2 * TP,)),
            pltpu.SemaphoreType.DMA((1,)),
        ],
    )(a, b)


def swap(slots):
    return lax.all_to_all(slots, "ctx", split_axis=0, concat_axis=0, tiled=True)


def dot(a, b):
    return lax.dot_general(a, b, (((1,), (0,)), ((), ())), preferred_element_type=F32)


def dot_t(a, b):
    return lax.dot_general(a, b, (((1,), (1,)), ((), ())), preferred_element_type=F32)


def dot_n(a, b):
    return lax.dot_general(a, b, (((0,), (0,)), ((), ())), preferred_element_type=F32)


STEP = 2
WIDE = STEP * HEAD_DIM
PAIR = pl.BlockSpec((2, ROWS, WIDE), lambda j, tab: (0, 0, j))
SECOND = pl.BlockSpec((1, ROWS, WIDE), lambda j, tab: (1, 0, j))
HEADS_ONE = pl.BlockSpec((ROWS, WIDE), lambda j, tab: (0, j))
PIECE = pl.BlockSpec((TOK, WIDE), lambda j, tab: (0, j))
PROBS = pl.BlockSpec((2, STEP, BLOCK, 2 * BLOCK), lambda j, tab: (0, j, 0, 0))
STATS = pl.BlockSpec((2, STEP, 8, BLOCK), lambda j, tab: (0, j, 0, 0))


def far_spec(n, u):
    return pl.BlockSpec(
        (1, BLOCK, HEAD_DIM), lambda j, tab: (tab[4, n * GROUPS + j * STEP + u], 0, 0)
    )


def half_spec(n, u):
    return pl.BlockSpec(
        (1, 2, HALF, HEAD_DIM), lambda j, tab: (tab[4, n * GROUPS + j * STEP + u], 0, 0, 0)
    )


def woven(first, second):
    return jnp.concatenate([first[0, 0], second[0, 0], first[0, 1], second[0, 1]], axis=0)


LANES = [(u, n) for u in range(STEP) for n in range(2)]
FAR = [far_spec(n, u) for u, n in LANES]
HALVES = [half_spec(n, u) for u, n in LANES]
LOW, HIGH = pl.ds(0, BLOCK), pl.ds(BLOCK, BLOCK)


def lanes(j):
    for index, (u, n) in enumerate(LANES):
        yield index, u, n, j * STEP + u, pl.ds(n * BLOCK, BLOCK), pl.ds(u * HEAD_DIM, HEAD_DIM)


def by_group(kernel, out_shape, in_specs, out_specs, scratch, free=()):
    def run(tab, *operands):
        outs = [pltpu.HBM(out.shape, out.dtype) for out in out_shape]
        operands = [
            x if index in free else pltpu.with_memory_space_constraint(x, pltpu.HBM)
            for index, x in enumerate(operands)
        ]
        return pl.pallas_call(
            kernel,
            out_shape=outs,
            grid_spec=pltpu.PrefetchScalarGridSpec(
                num_scalar_prefetch=1,
                grid=(GROUPS // STEP,),
                in_specs=in_specs,
                out_specs=out_specs,
                scratch_shapes=scratch,
            ),
            compiler_params=PARAMS,
        )(tab, *operands)

    return run


def matched(tab, g, n, received, low):
    if n == 0:
        return received
    return jnp.where(tab[3, GROUPS + g] == 2, low, received)


def prob_kernel(tab, kq, dout, *refs):
    count = len(FAR)
    first, second, (prob, lse_out, gv) = refs[:count], refs[count : 2 * count], refs[2 * count :]
    causal = lax.broadcasted_iota(jnp.int32, (BLOCK, BLOCK), 0) >= lax.broadcasted_iota(
        jnp.int32, (BLOCK, BLOCK), 1
    )
    for index, u, n, g, rows, cols in lanes(pl.program_id(0)):
        q = kq[1, rows, cols]
        kf = matched(tab, g, n, woven(first[index], second[index]), kq[0, LOW, cols])
        s_own = jnp.where(causal, dot_t(q, kq[0, rows, cols]) * SCALE, -jnp.inf)
        s_far = jnp.where(tab[3, n * GROUPS + g] > 0, dot_t(q, kf) * SCALE, -jnp.inf)
        top = jnp.maximum(
            jnp.max(s_own, axis=1, keepdims=True), jnp.max(s_far, axis=1, keepdims=True)
        )
        e_own = jnp.exp(s_own - top)
        e_far = jnp.exp(s_far - top)
        total = jnp.sum(e_own, axis=1, keepdims=True) + jnp.sum(e_far, axis=1, keepdims=True)
        inverse = 1.0 / total
        p_own = (e_own * inverse).astype(BF16)
        prob[n, u, :, LOW] = p_own
        prob[n, u, :, HIGH] = (e_far * inverse).astype(BF16)
        gv[rows, cols] = dot_n(p_own, dout[0, rows, cols])
        lse = jnp.broadcast_to(top + jnp.log(total), (BLOCK, HEAD_DIM))
        lse_out[n, u] = jnp.transpose(lse)[0:8]
    for index, u, n, g, rows, cols in lanes(pl.program_id(0)):
        if n == 1:

            @pl.when(tab[3, GROUPS + g] == 2)
            def _():
                gv[LOW, cols] += dot_n(prob[1, u, :, HIGH], dout[0, HIGH, cols])


def prob_side(tab, kq, vd, slots_a, slots_b):
    return by_group(
        prob_kernel,
        [
            shape((2, GROUPS, BLOCK, 2 * BLOCK)),
            shape((2, GROUPS, 8, BLOCK), F32),
            shape((ROWS, COLS), F32),
        ],
        [PAIR, SECOND] + HALVES * 2,
        [PROBS, STATS, HEADS_ONE],
        [],
    )(tab, kq, vd, *[slots_a] * len(FAR), *[slots_b] * len(FAR))


def piece_copies(result, outs, sems):
    return [
        pltpu.make_async_copy(result.at[row_slice(peer(move))], out, sems.at[move])
        for move, out in enumerate(outs)
    ]


def start_all(copies):
    for copy in copies:
        copy.start()


def wait_all(copies):
    for copy in copies:
        copy.wait()


def value_kernel(tab, prob, lse, vd, *refs):
    far, (own, p1, p2, p3, full, stats_slots, stats, slot_sems) = (
        refs[: len(FAR)],
        refs[len(FAR) :],
    )
    j = pl.program_id(0)
    ctx = lax.axis_index("ctx")
    sublane = lax.broadcasted_iota(jnp.int32, (8, BLOCK), 0)
    for index, u, n, g, rows, cols in lanes(j):
        vf = matched(tab, g, n, far[index][0], vd[0, LOW, cols])
        att = dot(prob[n, u, :, LOW], vd[0, rows, cols]) + dot(prob[n, u, :, HIGH], vf)
        att = att.astype(BF16)
        full[rows, cols] = att
        delta = jnp.sum(vd[1, rows, cols].astype(F32) * att.astype(F32), axis=1, keepdims=True)
        turned = jnp.transpose(jnp.broadcast_to(delta, (BLOCK, HEAD_DIM)))[0:8]
        stats[n * GROUPS + g] = jnp.where(sublane == 0, lse[n, u], turned)
    for move, out in enumerate((own, p1, p2, p3)):
        out[...] = full[row_slice(peer(move))]

    @pl.when(j == GROUPS // STEP - 1)
    def _():
        copies = []
        for d in range(CTX):
            item = jnp.where(ctx > d, tab[0, d] * GROUPS + tab[1, d], 0)
            copies.append(
                pltpu.make_async_copy(stats.at[item], stats_slots.at[d], slot_sems.at[d])
            )
        run_copies(copies)


def value_side(tab, prob, lse, vd, slots):
    return by_group(
        value_kernel,
        [shape((TOK, COLS))] * 4 + [shape((ROWS, COLS)), shape((CTX, 8, BLOCK), F32)],
        [PROBS, STATS, PAIR] + FAR,
        [PIECE] * 4 + [HEADS_ONE, HBM],
        [pltpu.VMEM((ITEMS, 8, BLOCK), F32), pltpu.SemaphoreType.DMA((CTX,))],
        free=range(3, 3 + len(FAR)),
    )(tab, prob, lse, vd, *[slots] * len(FAR))


def query_kernel(tab, prob, kq, vd, att, *refs):
    count = len(FAR)
    first, second, far_v = refs[:count], refs[count : 2 * count], refs[2 * count : 3 * count]
    own, p1, p2, p3, gk, result, ds_last = refs[3 * count :]
    for index, u, n, g, rows, cols in lanes(pl.program_id(0)):
        do = vd[1, rows, cols]
        kf = matched(tab, g, n, woven(first[index], second[index]), kq[0, LOW, cols])
        vf = matched(tab, g, n, far_v[index][0], vd[0, LOW, cols])
        delta = jnp.sum(do.astype(F32) * att[rows, cols].astype(F32), axis=1, keepdims=True)
        p_own = prob[n, u, :, LOW].astype(F32)
        p_far = prob[n, u, :, HIGH].astype(F32)
        ds_own = (p_own * (dot_t(do, vd[0, rows, cols]) - delta) * SCALE).astype(BF16)
        ds_far = (p_far * (dot_t(do, vf) - delta) * SCALE).astype(BF16)
        result[rows, cols] = (dot(ds_own, kq[0, rows, cols]) + dot(ds_far, kf)).astype(BF16)
        gk[rows, cols] = dot_n(ds_own, kq[1, rows, cols])
        if n == 1:
            ds_last[u] = ds_far
    for move, out in enumerate((own, p1, p2, p3)):
        out[...] = result[row_slice(peer(move))]
    for index, u, n, g, rows, cols in lanes(pl.program_id(0)):
        if n == 1:

            @pl.when(tab[3, GROUPS + g] == 2)
            def _():
                gk[LOW, cols] += dot_n(ds_last[u], kq[1, HIGH, cols])


def query_side(tab, prob, kq, vd, att, slots_a, slots_b, slots2):
    return by_group(
        query_kernel,
        [shape((TOK, COLS))] * 4 + [shape((ROWS, COLS), F32)],
        [PROBS, PAIR, PAIR, HEADS_ONE] + HALVES * 2 + FAR,
        [PIECE] * 4 + [HEADS_ONE],
        [pltpu.VMEM((ROWS, WIDE), BF16), pltpu.VMEM((STEP, BLOCK, BLOCK), BF16)],
    )(
        tab, prob, kq, vd, att,
        *[slots_a] * len(FAR), *[slots_b] * len(FAR), *[slots2] * len(FAR),
    )


def key_terms(k, v, q, do, stats):
    p = jnp.exp(dot_t(k, q) * SCALE - stats[0:1])
    ds = (p * (dot_t(v, do) - stats[1:2]) * SCALE).astype(BF16)
    return dot(ds, q), dot(p.astype(BF16), do)


JOBS = 4


def far_kernel(
    tab, kq_ref, vd_ref, slots_a, slots_b, slots2, stats, gk_ref, gv_ref,
    ko, k1, k2, k3, vo, v1, v2, v3,
    k, v, far_q, far_do, near, acc, result, sems, slot_sems, out_sems,
):
    ctx = lax.axis_index("ctx")

    def slot_copies(d):
        return [
            pltpu.make_async_copy(slots_a.at[d], far_q.at[d, :, 0], slot_sems.at[0, d]),
            pltpu.make_async_copy(slots_b.at[d], far_q.at[d, :, 1], slot_sems.at[1, d]),
            pltpu.make_async_copy(slots2.at[d], far_do.at[d], slot_sems.at[2, d]),
        ]

    def start_slot(d, carry):
        start_all(slot_copies(d))
        return carry

    loads = [
        pltpu.make_async_copy(kq_ref.at[0], k, sems.at[0]),
        pltpu.make_async_copy(vd_ref.at[0], v, sems.at[1]),
    ]
    near_loads = [
        pltpu.make_async_copy(gk_ref, near.at[0], sems.at[2]),
        pltpu.make_async_copy(gv_ref, near.at[1], sems.at[3]),
    ]
    start_all(loads)
    rounds = (CTX - 1 - ctx + JOBS - 1) // JOBS
    lax.fori_loop(0, JOBS * rounds, lambda j, c: start_slot((ctx + 1 + j) % CTX, c), 0)
    start_all(near_loads)
    acc[...] = jnp.zeros_like(acc)
    wait_all(loads)

    def step(turn, carry):
        picked = []
        for job in range(JOBS):
            want = ctx + 1 + JOBS * turn + job
            d = want % CTX
            wait_all(slot_copies(d))
            picked.append((d, (tab[2, d] == 1) & (want < CTX)))
        terms = []
        for d, filled in picked:
            rows, cols = block_slice(tab[0, d]), head_slice(tab[1, d])
            k_term, v_term = key_terms(
                k[rows, cols], v[rows, cols], far_q[d].reshape(BLOCK, HEAD_DIM), far_do[d], stats[d]
            )
            terms.append(
                (rows, cols, jnp.where(filled, k_term, 0.0), jnp.where(filled, v_term, 0.0))
            )
        for rows, cols, k_term, v_term in terms:
            acc[0, rows, cols] += k_term
            acc[1, rows, cols] += v_term
        return carry

    lax.fori_loop(0, rounds, step, 0)
    outs = ((ko, k1, k2, k3), (vo, v1, v2, v3))
    stores = []
    for which in range(2):
        near_loads[which].wait()
        result[which] = (near[which] + acc[which]).astype(BF16)
        copies = piece_copies(result.at[which], outs[which], out_sems.at[which])
        start_all(copies)
        stores += copies
    wait_all(stores)


def far_side(tab, kq, vd, slots_a, slots_b, slots2, stats, gk, gv):
    return call(
        far_kernel,
        [shape((TOK, COLS))] * 8,
        [SMEM] + [HBM] * 5 + [VMEM] + [HBM] * 2,
        [HBM] * 8,
        [
            pltpu.VMEM((ROWS, COLS), BF16),
            pltpu.VMEM((ROWS, COLS), BF16),
            pltpu.VMEM((CTX, 2, 2, HALF, HEAD_DIM), BF16),
            pltpu.VMEM((CTX, BLOCK, HEAD_DIM), BF16),
            pltpu.VMEM((2, ROWS, COLS), F32),
            pltpu.VMEM((2, ROWS, COLS), F32),
            pltpu.VMEM((2, ROWS, COLS), BF16),
            pltpu.SemaphoreType.DMA((4,)),
            pltpu.SemaphoreType.DMA((3, CTX)),
            pltpu.SemaphoreType.DMA((2, TP)),
        ],
    )(tab, kq, vd, slots_a, slots_b, slots2, stats, gk, gv)


def shards(queries, keys, values, dout, match):
    ka_in = exchange(cut(keys, queries, 0, HALF))
    kb_in = exchange(cut(keys, queries, HALF, HALF))
    vd_in = exchange(cut(values, dout, 0, TOK))
    tab = make_table(match)
    slots_a, held_a = pack(tab, keys, queries, ka_in, 0, HALF)
    far_a = swap(slots_a)
    slots_b, held_b = pack(tab, keys, queries, kb_in, HALF, HALF)
    slots_b, far_a = lax.optimization_barrier((slots_b, far_a))
    far_b = swap(slots_b)
    slots2, vd = pack(tab, values, dout, vd_in, 0, TOK)
    slots2, far_b = lax.optimization_barrier((slots2, far_b))
    far2 = swap(slots2)
    kq = hold(held_a, held_b)
    far_a = far_a.reshape(CTX, 2, HALF, HEAD_DIM)
    far_b = far_b.reshape(CTX, 2, HALF, HEAD_DIM)
    prob, lse, gv = prob_side(tab, kq, vd, far_a, far_b)
    *att, att_full, stats_slots = value_side(tab, prob, lse, vd, far2)
    att_in = exchange(att[1:4])
    far_stats = swap(stats_slots)
    *gq, gk = query_side(tab, prob, kq, vd, att_full, far_a, far_b, far2)
    gq_in = exchange(gq[1:4])
    out = far_side(tab, kq, vd, far_a, far_b, far2, far_stats, gk, gv)
    gk_in = exchange(out[1:4])
    gv_in = exchange(out[5:])
    return (join(att[0], att_in), join(gq[0], gq_in), join(out[0], gk_in), join(out[4], gv_in))


def solution(mesh):
    placed = P(("ctx", "tp"), None)
    return jax.shard_map(
        shards,
        mesh=mesh,
        in_specs=(placed, placed, placed, placed, P()),
        out_specs=(placed, placed, placed, placed),
        check_vma=False,
    )
```
